512 devices in a mesh: gx: 32 (over x, z), gy: 16 (over y, core).
Axes of the slice: x: 4, y: 8, z: 8, core: 2. Of those that a mesh axis runs over, the one named last changes fastest.
Arguments:
- seeds: int32 [64, 1024], P('gy', 'gx'), may hold values from 0 to 1073741823
- lengths: float32 [3], replicated, may hold values from 3 to 24
- exponents: float32 [3], replicated, may hold values from 1.5 to 2.5
- storage: float32 [64, 1024, 1024], P('gy', 'gx'), may hold values from 0.5 to 8
- recharge: float32 [64, 1024, 1024], P('gy', 'gx'), may hold values from -36 to 36
- well_cells: int32 [3, 256], replicated, may hold values from 0 to 1023, as said below
- well_rates: float32 [256], replicated, may hold values from -180 to 180
Outputs:
- log_perm: float32 [64, 1024, 1024], P('gy', 'gx')
- pressure: float32 [64, 1024, 1024], P('gy', 'gx')
- residual: float32 [64, 1024, 1024], P('gy', 'gx')
The draws below stay inside these ranges and needn't reach their ends.
Inputs may be any that keep to these rules, and one draw needn't show every extreme that they name: Row 0 of well_cells gives each well's layer, below 64; rows 1 and 2 its cell along the second and third dimensions, below 1024 and 1024. Wells may share a cell; their rates then add.
All inputs are finite; a program needn't handle non-finite values.
Results may differ from the reference program's by a relative error of at most 0.00024.
Values sent between devices are 32-bit elements; how exact they have to be, the bound alone decides.
No kernel may reach another device: no remote copies, remote signals or barrier semaphores. Data moves between devices by JAX's collectives and lax.ppermute only.
A program may use at most 128 MiB of HBM per device.

```python
import math
import jax
import jax.numpy as jnp

LZ = 64
LX = 1024
LY = 1024
WELLS = 256
ITERS = 3


def draw_well_cells(key, part):
    keys = jax.random.split(key, 3)
    layer = jax.random.randint(keys[0], (WELLS,), 0, LZ, dtype=jnp.int32)
    row_cell = jax.random.randint(keys[1], (WELLS,), 0, LX, dtype=jnp.int32)
    column_cell = jax.random.randint(keys[2], (WELLS,), 0, LY, dtype=jnp.int32)
    layer = layer.at[0].set(LZ - 1)
    row_cell = row_cell.at[0].set(LX - 1).at[1].set(0)
    column_cell = column_cell.at[0].set(LY - 1)
    return jnp.stack([layer, row_cell, column_cell]).astype(jnp.int32)


def plant(drawn, rng, least, largest):
    index_at = [jax.random.randint(jax.random.fold_in(rng, axis), (), 0, length) for axis, length in enumerate(drawn.shape)]
    widest = drawn.shape.index(max(drawn.shape))
    neighbour = index_at[:widest] + [(index_at[widest] + 1) % drawn.shape[widest]] + index_at[widest + 1:]
    return drawn.at[tuple(index_at)].set(least).at[tuple(neighbour)].set(largest)


def block_levels(own_key, extent, cuts, least, largest):
    level = 1.0
    for axis_at, blocks in cuts:
        steps = jax.random.uniform(jax.random.fold_in(jax.random.fold_in(own_key, 6), axis_at), (blocks,), jnp.float32, least / len(cuts), largest / len(cuts))
        level = level * jnp.repeat(jnp.exp(steps), extent[axis_at] // blocks).reshape((-1,) + (1,) * (len(extent) - 1 - axis_at))
    return level


def normal_values(rng, extent, width, bound, pieces=(), held_as=jnp.bfloat16):
    drawn = jax.random.normal(rng, extent, jnp.float32) * width
    if len(pieces) > 0:
        drawn = block_levels(rng, extent, pieces, -0.22, 0.18) * drawn
    return jnp.clip(drawn, min=-bound, max=bound).astype(held_as)


def setup_inputs(seed: int = 0) -> dict:
    key_list = jax.random.split(jax.random.key(seed), 8)
    return {
        "seeds": plant(jax.random.randint(key_list[0], (LZ, LX), 0, 1073741824), jax.random.fold_in(key_list[0], 1), 0, 1073741823).astype(jnp.int32),
        "lengths": jnp.clip(jnp.exp(jax.random.uniform(key_list[1], (3,), jnp.float32, math.log(3.0), math.log(24.0))), 3.0, 24.0),
        "exponents": jnp.clip(jax.random.uniform(key_list[2], (3,), jnp.float32, 1.5, 2.5), 1.5, 2.5),
        "storage": jnp.clip(jnp.exp(math.log(8.0) - 2.7725887 * jax.random.uniform(key_list[3], (LZ, LX, LY), jnp.float32) ** block_levels(key_list[3], (LZ, LX, LY), ((0, 16), (1, 32)), -0.2, 0.2)), 0.5, 8.0),
        "recharge": normal_values(key_list[4], (LZ, LX, LY), 6.0, 36.0, ((0, 16), (1, 32)), jnp.float32),
        "well_cells": draw_well_cells(jax.random.fold_in(key_list[7], 71), 0),
        "well_rates": normal_values(key_list[6], (WELLS,), 30.0, 180.0, (), jnp.float32),
    }


AMPLITUDE = 4.0

def mix_bits(seed_rows, cells):
    hashed = seed_rows + cells * jnp.int32(-1640531535)
    hashed = hashed ^ hashed >> 16 & 65535
    hashed = hashed * jnp.int32(-2048144789)
    hashed = hashed ^ hashed >> 13 & 524287
    hashed = hashed * jnp.int32(-1028477387)
    hashed = hashed ^ hashed >> 16 & 65535
    value = (hashed >> 8 & 16777215).astype(jnp.float32)
    return (value + 0.5) * (2.0 * math.sqrt(3.0) / 16777216.0) - math.sqrt(3.0)

def magnitude(index, length):
    folded = jnp.minimum(index, length - index)
    return folded.astype(jnp.float32) * (2.0 * math.pi / length)

def filter_gain(wave_z, wave_x, wave_y, lengths, exponents):
    total = 1.0 + jnp.power(lengths[0] * wave_z, exponents[0])
    total = total + jnp.power(lengths[1] * wave_x, exponents[1])
    total = total + jnp.power(lengths[2] * wave_y, exponents[2])
    return AMPLITUDE * jnp.sqrt(lengths[0] * lengths[1] * lengths[2]) / total

def harmonic(centre, other):
    return 2.0 * centre * other / (centre + other)

def neighbours(padded):
    centre = padded[1:-1, 1:-1, :]
    y_low = jnp.pad(centre[:, :, :-1], ((0, 0), (0, 0), (1, 0)))
    y_high = jnp.pad(centre[:, :, 1:], ((0, 0), (0, 0), (0, 1)))
    return [padded[:-2, 1:-1, :], padded[2:, 1:-1, :], padded[1:-1, :-2, :], padded[1:-1, 2:, :], y_low, y_high]

def pad_plane(field):
    return jnp.pad(field, ((1, 1), (1, 1), (0, 0)))

def apply_operator(field, perm_near, perm, storage):
    result = storage * field
    for perm_other, other in zip(neighbours(perm_near), neighbours(pad_plane(field))):
        result = result + harmonic(perm, perm_other) * (field - other)
    return result

def reference(seeds, lengths, exponents, storage, recharge, well_cells, well_rates):
    cells = jnp.arange(LY, dtype=jnp.int32)
    noise = mix_bits(seeds[:, :, None], cells[None, None, :])
    spectrum = jnp.fft.rfftn(noise)
    wave_z = magnitude(jnp.arange(LZ, dtype=jnp.int32), LZ)
    wave_x = magnitude(jnp.arange(LX, dtype=jnp.int32), LX)
    y_index = jnp.arange(LY // 2 + 1, dtype=jnp.int32)
    wave_y = magnitude(y_index, LY)
    keep_y = (y_index != LY // 2).astype(jnp.float32)
    gain = filter_gain(wave_z[:, None, None], wave_x[None, :, None], wave_y[None, None, :], lengths, exponents)
    gain = gain * keep_y[None, None, :]
    log_perm = jnp.fft.irfftn(spectrum * gain, s=(LZ, LX, LY)).astype(jnp.float32)
    perm = jnp.exp(log_perm)
    perm_near = pad_plane(perm)
    diag = storage
    for other in neighbours(perm_near):
        diag = diag + harmonic(perm, other)
    rhs = recharge.at[well_cells[0], well_cells[1], well_cells[2]].add(well_rates)
    pressure = jnp.zeros_like(rhs)
    residual = rhs
    precond = residual / diag
    direction = precond
    rz_now = jnp.sum(residual * precond)
    for step in range(ITERS):
        image = apply_operator(direction, perm_near, perm, storage)
        alpha = rz_now / jnp.sum(direction * image)
        pressure = pressure + alpha * direction
        residual = residual - alpha * image
        precond = residual / diag
        rz_next = jnp.sum(residual * precond)
        direction = precond + rz_next / rz_now * direction
        rz_now = rz_next
    return (log_perm, pressure, residual)
```

```python
import math

import jax
import jax.numpy as jnp
import numpy as np
from jax import lax
from jax.experimental import pallas as pl
from jax.experimental.pallas import tpu as pltpu
from jax.sharding import PartitionSpec as P

AMPLITUDE = 4.0
BF16 = jnp.bfloat16
F32 = jnp.float32
INTERPRET = False


def call(body, outs, *args, specs=None):
    return pl.pallas_call(
        body,
        out_shape=outs,
        in_specs=specs or [pl.BlockSpec(memory_space=pltpu.VMEM)] * len(args),
        interpret=INTERPRET,
        compiler_params=pltpu.CompilerParams(vmem_limit_bytes=60 * 2**20),
    )(*args)


def f32(*shape):
    return jax.ShapeDtypeStruct(shape, F32)


def halves(table):
    high = table.astype(BF16)
    low = (table - high.astype(np.float64)).astype(BF16)
    return jnp.asarray(high), jnp.asarray(low)


def cosine_sine(product, length):
    angle = (product % length).astype(np.float64) * (2.0 * math.pi / length)
    return np.cos(angle), np.sin(angle)


def table_y(length):
    half = length // 2
    k = np.concatenate([np.arange(0, half, 2), np.arange(1, half, 2)])
    cos, sin = cosine_sine(k[:, None] * np.arange(half)[None, :], length)
    return np.stack([cos, -sin], axis=1).reshape(2 * half, half)


def tables_zx(gx, gy, zl, xl):
    row_x, row_z = np.repeat(np.arange(gx), gy), np.tile(np.arange(gy), gx)
    col_x, col_z = np.tile(np.arange(xl), zl), np.repeat(np.arange(zl), xl)

    def table(left_x, right_x, left_z, right_z, size_x, size_z):
        phase = np.outer(left_x, right_x) / size_x + np.outer(left_z, right_z) / size_z
        return np.exp(-2j * math.pi * phase)

    outer = table(row_x, row_x, row_z, row_z, gx, gy)
    twiddle = table(row_x, col_x, row_z, col_z, gx * xl, gy * zl)
    inner = table(col_x, col_x, col_z, col_z, xl, zl)
    forward = np.block([[inner.real, inner.imag], [-inner.imag, inner.real]])
    return outer, twiddle, forward


def split(data):
    high = data.astype(BF16)
    return high, (data - high.astype(F32)).astype(BF16)


def dot(a, b):
    return jnp.dot(a, b, preferred_element_type=F32)


def left_product(table, data):
    (th, tl), (dh, dl) = table, data
    return dot(th, dh) + (dot(th, dl) + dot(tl, dh))


def right_product(data, table):
    (dh, dl), (th, tl) = data, table
    return dot(dh, th) + (dot(dl, th) + dot(dh, tl))


def mix_bits(seed_rows, cells):
    shift = lax.shift_right_logical
    hashed = seed_rows + cells * jnp.int32(-1640531535)
    hashed = hashed ^ shift(hashed, jnp.int32(16))
    hashed = hashed * jnp.int32(-2048144789)
    hashed = hashed ^ shift(hashed, jnp.int32(13))
    hashed = hashed * jnp.int32(-1028477387)
    hashed = hashed ^ shift(hashed, jnp.int32(16))
    value = shift(hashed, jnp.int32(8)).astype(F32)
    return (value + 0.5) * (2.0 * math.sqrt(3.0) / 16777216.0) - math.sqrt(3.0)


def noise_kernel(seed_ref, th_ref, tl_ref, out_ref):
    rows, half = th_ref.shape
    seeds = seed_ref[...]
    cells = lax.broadcasted_iota(jnp.int32, (half, seeds.shape[1]), 0)
    near = mix_bits(seeds, cells)
    far = mix_bits(seeds, cells + half)
    mid = rows // 2
    out_ref[:mid] = left_product((th_ref[:mid], tl_ref[:mid]), split(near + far))
    out_ref[mid:] = left_product((th_ref[mid:], tl_ref[mid:]), split(near - far))


def power(base, exponent):
    return jnp.exp(exponent * jnp.log(base))


def spectrum_kernel(sizes, device_ref, lengths_ref, exponents_ref, data_ref, ar_h, ar_l, ai_h, ai_l, tr_ref, ti_ref, fh_ref, fl_ref, gh_ref, gl_ref, out_ref):
    gx, gy, zl, xl, length_y = sizes
    rows, cols = gx * gy, zl * xl
    outer_r = (ar_h[...], ar_l[...])
    outer_i = (ai_h[...], ai_l[...])
    tr, ti = tr_ref[...], ti_ref[...]
    shape = (rows, cols)
    row = lax.broadcasted_iota(jnp.int32, shape, 0)
    col = lax.broadcasted_iota(jnp.int32, shape, 1)
    kx = lax.div(row, gy) + gx * lax.rem(col, xl)
    kz = lax.rem(row, gy) + gy * lax.div(col, xl)
    device = device_ref[0]
    half_rows = rows // 2
    ky = jnp.where(device < half_rows, 2 * device, 2 * (device - half_rows) + 1)

    def wave(index, length):
        folded = jnp.minimum(index, length - index)
        return folded.astype(F32) * (2.0 * math.pi / length)

    ky_all = jnp.full((8, cols), ky, jnp.int32)
    total_y = 1.0 + power(lengths_ref[2] * wave(ky_all, length_y), exponents_ref[2])
    weight = jnp.where(ky_all == 0, 1.0, 2.0)
    volume = jnp.full((8, cols), lengths_ref[0] * lengths_ref[1] * lengths_ref[2], F32)
    scale = 1.0 / (gx * xl * gy * zl * length_y)
    numerator = AMPLITUDE * jnp.sqrt(volume) * scale * weight
    total = power(lengths_ref[0] * wave(kz, gy * zl), exponents_ref[0])
    total = total + power(lengths_ref[1] * wave(kx, gx * xl), exponents_ref[1])
    gain = numerator[:1] / (total_y[:1] + total)
    data = jnp.concatenate([data_ref[pl.ds(0, rows, stride=2), :], data_ref[pl.ds(1, rows, stride=2), :]], axis=1)
    parts = split(data)
    pr, pi = left_product(outer_r, parts), left_product(outer_i, parts)
    yr, yi = pr[:, :cols] - pi[:, cols:], pr[:, cols:] + pi[:, :cols]
    data = jnp.concatenate([yr * tr - yi * ti, yr * ti + yi * tr], axis=1)
    data = right_product(split(data), (fh_ref[...], fl_ref[...]))
    data = data * jnp.concatenate([gain, gain], axis=1)
    data = right_product(split(data), (gh_ref[...], gl_ref[...]))
    yr, yi = data[:, :cols], data[:, cols:]
    data = jnp.concatenate([yr * tr + yi * ti, yi * tr - yr * ti], axis=1)
    parts = split(data)
    pr, pi = left_product(outer_r, parts), left_product(outer_i, parts)
    out_ref[pl.ds(0, rows, stride=2), :] = pr[:, :cols] + pi[:, cols:]
    out_ref[pl.ds(1, rows, stride=2), :] = pr[:, cols:] - pi[:, :cols]


def faces(value, xl, refs):
    rows = value.shape[0]
    refs[0][...] = value[:xl]
    refs[1][...] = value[rows - xl :]
    for layer in range(rows // xl):
        refs[2][layer : layer + 1] = value[layer * xl : layer * xl + 1]
        refs[3][layer : layer + 1] = value[(layer + 1) * xl - 1 : (layer + 1) * xl]


def field_kernel(xl, data_ref, th_ref, tl_ref, log_ref, perm_ref, *face_refs):
    rows, half = th_ref.shape
    mid = rows // 2
    turned = jnp.transpose(data_ref[...])
    even = right_product(split(turned[:, :mid]), (th_ref[:mid], tl_ref[:mid]))
    odd = right_product(split(turned[:, mid:]), (th_ref[mid:], tl_ref[mid:]))
    log_ref[:, :half] = even + odd
    log_ref[:, half:] = even - odd
    perm = jnp.exp(log_ref[...])
    perm_ref[...] = perm
    faces(perm, xl, face_refs)


def shifted(value, halo, xl):
    z_low, z_high, x_low, x_high = halo
    rows, length = value.shape
    layers = rows // xl
    place = lax.broadcasted_iota(jnp.int32, (xl, length), 0)
    lows, highs = [], []
    for layer in range(layers):
        block = value[layer * xl : (layer + 1) * xl]
        lows.append(jnp.where(place == 0, x_low[layer : layer + 1], pltpu.roll(block, 1, 0)))
        highs.append(jnp.where(place == xl - 1, x_high[layer : layer + 1], pltpu.roll(block, xl - 1, 0)))
    return (
        jnp.concatenate([z_low, value[: rows - xl]], axis=0),
        jnp.concatenate([value[xl:], z_high], axis=0),
        jnp.concatenate(lows, axis=0),
        jnp.concatenate(highs, axis=0),
        pltpu.roll(value, 1, 1),
        pltpu.roll(value, length - 1, 1),
    )


def lane_sum(value, lane_at):
    total = jnp.sum(jnp.sum(value, axis=0, keepdims=True), axis=1, keepdims=True)
    lane = lax.broadcasted_iota(jnp.int32, (1, 128), 1)
    return jnp.where(lane == lane_at, total, 0.0)


def rhs_kernel(origin_ref, recharge_ref, cells_ref, rates_ref, rhs_ref, *, xl):
    rows, length = recharge_ref.shape
    wells = cells_ref.shape[1]
    layer = cells_ref[0:1] - origin_ref[0]
    line = cells_ref[1:2] - origin_ref[1]
    inside = (line >= 0) & (line < xl)
    at = jnp.where(inside, layer * xl + line, -1)
    rate = jnp.where(lax.broadcasted_iota(jnp.int32, (rows, wells), 0) == at, rates_ref[...], 0.0)
    column = (lax.broadcasted_iota(jnp.int32, (length, wells), 0) == cells_ref[2:3]).astype(F32).astype(BF16)
    added = None
    for _ in range(3):
        part = rate.astype(BF16)
        rate = rate - part.astype(F32)
        product = lax.dot_general(part, column, (((1,), (1,)), ((), ())), preferred_element_type=F32)
        added = product if added is None else added + product
    rhs_ref[...] = recharge_ref[...] + added


def setup_kernel(xl, perm_ref, h0, h1, h2, h3, storage_ref, rhs_ref, c0, c1, c2, c3, c4, c5, diag_ref, u_ref, f0, f1, f2, f3, mom_ref):
    perm = perm_ref[...]
    length = perm.shape[1]
    place = lax.broadcasted_iota(jnp.int32, perm.shape, 1)
    around = list(shifted(perm, (h0[...], h1[...], h2[...], h3[...]), xl))
    around[4] = jnp.where(place == 0, 0.0, around[4])
    around[5] = jnp.where(place == length - 1, 0.0, around[5])
    twice = 2.0 * perm
    flows = [twice * other / (perm + other) for other in around]
    diag = storage_ref[...]
    for flow in flows:
        diag = diag + flow
    inverse = 1.0 / diag
    for ref, flow in zip((c0, c1, c2, c3, c4, c5), flows):
        ref[...] = flow * inverse
    rhs = rhs_ref[...]
    u = rhs * inverse
    diag_ref[...] = diag
    u_ref[...] = u
    faces(u, xl, (f0, f1, f2, f3))
    mom_ref[...] = lane_sum(rhs * u, 0)


def step_kernel(xl, at, last, u_ref, h0, h1, h2, h3, c0, c1, c2, c3, c4, c5, diag_ref, mom_in, new_ref, *rest):
    around = shifted(u_ref[...], (h0[...], h1[...], h2[...], h3[...]), xl)
    new = None
    for coef, other in zip((c0, c1, c2, c3, c4, c5), around):
        term = coef[...] * other
        new = term if new is None else new + term
    new_ref[...] = new
    weighted = diag_ref[...] * new
    mom = mom_in[...] + lane_sum(weighted * u_ref[...], at)
    if last:
        rest[0][...] = jnp.broadcast_to(mom, rest[0].shape)
    else:
        faces(new, xl, rest[:4])
        rest[4][...] = mom + lane_sum(weighted * new, at + 1)


def partial_kernel(in_ref, out_ref):
    out_ref[...] = jnp.broadcast_to(jnp.sum(in_ref[...], axis=0, keepdims=True), out_ref.shape)


def final_kernel(iters, mom_ref, u0, u1, u2, u3, diag_ref, pressure_ref, residual_ref):
    moments = jnp.sum(mom_ref[...], axis=0, keepdims=True)
    lane = lax.broadcasted_iota(jnp.int32, (1, 128), 1)
    nu = [jnp.sum(jnp.where(lane == i, moments, 0.0), axis=1, keepdims=True) for i in range(2 * iters)]

    def form(a, b):
        total = None
        for i, left in enumerate(a):
            for j, right in enumerate(b):
                term = left * right * nu[i + j]
                total = term if total is None else total + term
        return total

    one = jnp.ones((1, 1), F32)
    zero = jnp.zeros((1, 1), F32)
    precond, direction, pressure = [one], [one], [zero] * iters
    rz = nu[0]
    for it in range(iters):
        image = [
            (direction[i] if i < len(direction) else zero) - (direction[i - 1] if i > 0 else zero)
            for i in range(len(direction) + 1)
        ]
        alpha = rz / form(direction, image)
        pressure = [old + alpha * direction[i] if i < len(direction) else old for i, old in enumerate(pressure)]
        precond = [(precond[i] if i < len(precond) else zero) - alpha * image[i] for i in range(len(image))]
        if it + 1 < iters:
            new = form(precond, precond)
            beta = new / rz
            direction = [
                precond[i] + beta * direction[i] if i < len(direction) else precond[i] for i in range(len(precond))
            ]
            rz = new
    basis = [u0[...], u1[...], u2[...], u3[...]]
    pressure_ref[...] = pressure[0] * basis[0] + pressure[1] * basis[1] + pressure[2] * basis[2]
    total = precond[0] * basis[0] + precond[1] * basis[1] + precond[2] * basis[2] + precond[3] * basis[3]
    residual_ref[...] = diag_ref[...] * total


ITERS = 3


def exchange(face):
    out = []
    for axis, low, high in (("gy", face[0], face[1]), ("gx", face[2], face[3])):
        count = lax.axis_size(axis)
        up = [(i, i + 1) for i in range(count - 1)]
        down = [(i + 1, i) for i in range(count - 1)]
        out.append(lax.ppermute(high, axis, up))
        out.append(lax.ppermute(low, axis, down))
    return out


def shards(seeds, lengths, exponents, storage, recharge, well_cells, well_rates):
    zl, xl, length_y = storage.shape
    gx, gy = lax.axis_size("gx"), lax.axis_size("gy")
    rows = zl * xl
    block, zface, xface = f32(rows, length_y), f32(xl, length_y), f32(zl, length_y)
    face_shapes = [zface, zface, xface, xface]
    at_x, at_y = lax.axis_index("gx"), lax.axis_index("gy")
    device = (at_x * gy + at_y).reshape(1).astype(jnp.int32)
    origin = jnp.stack([at_y * zl, at_x * xl]).astype(jnp.int32)
    smem = pl.BlockSpec(memory_space=pltpu.SMEM)
    vmem = pl.BlockSpec(memory_space=pltpu.VMEM)
    ty = halves(table_y(length_y))
    outer, twiddle, inner = tables_zx(gx, gy, zl, xl)

    spectrum = call(noise_kernel, f32(length_y, rows), seeds.reshape(1, rows), *ty)
    rhs = call(
        lambda *refs: rhs_kernel(*refs, xl=xl),
        block,
        origin,
        recharge.reshape(rows, length_y),
        well_cells,
        well_rates.reshape(1, -1),
        specs=[smem, vmem, vmem, vmem],
    )

    def everywhere(array):
        return lax.all_to_all(array, ("gx", "gy"), split_axis=0, concat_axis=0, tiled=True)

    spectrum = everywhere(spectrum)
    spectrum = call(
        lambda *refs: spectrum_kernel((gx, gy, zl, xl, length_y), *refs),
        f32(length_y, rows),
        device,
        lengths,
        exponents,
        spectrum,
        *halves(outer.real),
        *halves(outer.imag),
        jnp.asarray(twiddle.real, F32),
        jnp.asarray(twiddle.imag, F32),
        *halves(inner),
        *halves(inner.T),
        specs=[smem, smem, smem] + [vmem] * 11,
    )
    spectrum = everywhere(spectrum)
    log_perm, perm, *face = call(
        lambda *refs: field_kernel(xl, *refs), [block, block] + face_shapes, spectrum, *ty
    )
    *coefs, diag, u0, f0, f1, f2, f3, moments = call(
        lambda *refs: setup_kernel(xl, *refs),
        [block] * 8 + face_shapes + [f32(1, 128)],
        perm,
        *exchange(face),
        storage.reshape(rows, length_y),
        rhs,
    )
    face = (f0, f1, f2, f3)
    basis = [u0]
    for step in range(ITERS):
        last = step + 1 == ITERS
        outs = [block, f32(gx, 128)] if last else [block] + face_shapes + [f32(1, 128)]
        new, *rest = call(
            lambda *refs, step=step, last=last: step_kernel(xl, 2 * step + 1, last, *refs),
            outs,
            basis[-1],
            *exchange(face),
            *coefs,
            diag,
            moments,
        )
        basis.append(new)
        face, moments = rest[:4], rest[-1]
    moments = lax.all_to_all(moments, "gx", split_axis=0, concat_axis=0, tiled=True)
    moments = call(partial_kernel, f32(gy, 128), moments)
    moments = lax.all_to_all(moments, "gy", split_axis=0, concat_axis=0, tiled=True)
    pressure, residual = call(
        lambda *refs: final_kernel(ITERS, *refs), [block, block], moments, *basis, diag
    )
    shape = storage.shape
    return (log_perm.reshape(shape), pressure.reshape(shape), residual.reshape(shape))


def solution(mesh):
    placed = (P("gy", "gx"), P(), P(), P("gy", "gx", None), P("gy", "gx", None), P(), P())
    return jax.shard_map(
        shards,
        mesh=mesh,
        in_specs=placed,
        out_specs=(P("gy", "gx", None), P("gy", "gx", None), P("gy", "gx", None)),
        check_vma=False,
    )
```

```python
import math

import jax
import jax.numpy as jnp
import numpy as np
from jax import lax
from jax.experimental import pallas as pl
from jax.experimental.pallas import tpu as pltpu
from jax.sharding import PartitionSpec as P

AMPLITUDE = 4.0
BF16 = jnp.bfloat16
F32 = jnp.float32
INTERPRET = False


def call(body, outs, *args, specs=None, scratch=()):
    return pl.pallas_call(
        body,
        out_shape=outs,
        in_specs=specs or [pl.BlockSpec(memory_space=pltpu.VMEM)] * len(args),
        scratch_shapes=scratch,
        interpret=INTERPRET,
        compiler_params=pltpu.CompilerParams(vmem_limit_bytes=60 * 2**20),
    )(*args)


def f32(*shape):
    return jax.ShapeDtypeStruct(shape, F32)


def halves(table):
    high = table.astype(BF16)
    low = (table - high.astype(np.float64)).astype(BF16)
    return jnp.asarray(high), jnp.asarray(low)


def cosine_sine(product, length):
    angle = (product % length).astype(np.float64) * (2.0 * math.pi / length)
    return np.cos(angle), np.sin(angle)


def table_y(length):
    half = length // 2
    k = np.concatenate([np.arange(0, half, 2), np.arange(1, half, 2)])
    cos, sin = cosine_sine(k[:, None] * np.arange(half)[None, :], length)
    return np.stack([cos, -sin], axis=1).reshape(2 * half, half)


def tables_zx(gx, gy, zl, xl):
    row_x, row_z = np.repeat(np.arange(gx), gy), np.tile(np.arange(gy), gx)
    col_x, col_z = np.tile(np.arange(xl), zl), np.repeat(np.arange(zl), xl)

    def table(left_x, right_x, left_z, right_z, size_x, size_z):
        phase = np.outer(left_x, right_x) / size_x + np.outer(left_z, right_z) / size_z
        return np.exp(-2j * math.pi * phase)

    outer = table(row_x, row_x, row_z, row_z, gx, gy)
    twiddle = table(row_x, col_x, row_z, col_z, gx * xl, gy * zl)
    inner = table(col_x, col_x, col_z, col_z, xl, zl)
    forward = np.block([[inner.real, inner.imag], [-inner.imag, inner.real]])
    return outer, twiddle, forward


def split(data):
    high = data.astype(BF16)
    return high, (data - high.astype(F32)).astype(BF16)


def dot(a, b):
    return jnp.dot(a, b, preferred_element_type=F32)


def left_product(table, data):
    (th, tl), (dh, dl) = table, data
    return dot(th, dh) + (dot(th, dl) + dot(tl, dh))


def right_product(data, table):
    (dh, dl), (th, tl) = data, table
    return dot(dh, th) + (dot(dl, th) + dot(dh, tl))


def mix_bits(seed_rows, cells):
    shift = lax.shift_right_logical
    hashed = seed_rows + cells * jnp.int32(-1640531535)
    hashed = hashed ^ shift(hashed, jnp.int32(16))
    hashed = hashed * jnp.int32(-2048144789)
    hashed = hashed ^ shift(hashed, jnp.int32(13))
    hashed = hashed * jnp.int32(-1028477387)
    hashed = hashed ^ shift(hashed, jnp.int32(16))
    value = shift(hashed, jnp.int32(8)).astype(F32)
    return (value + 0.5) * (2.0 * math.sqrt(3.0) / 16777216.0) - math.sqrt(3.0)


def noise_kernel(seed_ref, th_ref, tl_ref, out_ref):
    rows, half = th_ref.shape
    seeds = seed_ref[...]
    cells = lax.broadcasted_iota(jnp.int32, (half, seeds.shape[1]), 0)
    near = mix_bits(seeds, cells)
    far = mix_bits(seeds, cells + half)
    mid = rows // 2
    out_ref[:mid] = left_product((th_ref[:mid], tl_ref[:mid]), split(near + far))
    out_ref[mid:] = left_product((th_ref[mid:], tl_ref[mid:]), split(near - far))


def power(base, exponent):
    return jnp.exp(exponent * jnp.log(base))


def spectrum_kernel(sizes, device_ref, lengths_ref, exponents_ref, data_ref, ar_h, ar_l, ai_h, ai_l, tr_ref, ti_ref, fh_ref, fl_ref, gh_ref, gl_ref, out_ref):
    gx, gy, zl, xl, length_y = sizes
    rows, cols = gx * gy, zl * xl
    outer_r = (ar_h[...], ar_l[...])
    outer_i = (ai_h[...], ai_l[...])
    tr, ti = tr_ref[...], ti_ref[...]
    shape = (rows, cols)
    row = lax.broadcasted_iota(jnp.int32, shape, 0)
    col = lax.broadcasted_iota(jnp.int32, shape, 1)
    kx = lax.div(row, gy) + gx * lax.rem(col, xl)
    kz = lax.rem(row, gy) + gy * lax.div(col, xl)
    device = device_ref[0]
    half_rows = rows // 2
    ky = jnp.where(device < half_rows, 2 * device, 2 * (device - half_rows) + 1)

    def wave(index, length):
        folded = jnp.minimum(index, length - index)
        return folded.astype(F32) * (2.0 * math.pi / length)

    ky_all = jnp.full((8, cols), ky, jnp.int32)
    total_y = 1.0 + power(lengths_ref[2] * wave(ky_all, length_y), exponents_ref[2])
    weight = jnp.where(ky_all == 0, 1.0, 2.0)
    volume = jnp.full((8, cols), lengths_ref[0] * lengths_ref[1] * lengths_ref[2], F32)
    scale = 1.0 / (gx * xl * gy * zl * length_y)
    numerator = AMPLITUDE * jnp.sqrt(volume) * scale * weight
    total = power(lengths_ref[0] * wave(kz, gy * zl), exponents_ref[0])
    total = total + power(lengths_ref[1] * wave(kx, gx * xl), exponents_ref[1])
    gain = numerator[:1] / (total_y[:1] + total)
    data = jnp.concatenate([data_ref[pl.ds(0, rows, stride=2), :], data_ref[pl.ds(1, rows, stride=2), :]], axis=1)
    parts = split(data)
    pr, pi = left_product(outer_r, parts), left_product(outer_i, parts)
    yr, yi = pr[:, :cols] - pi[:, cols:], pr[:, cols:] + pi[:, :cols]
    data = jnp.concatenate([yr * tr - yi * ti, yr * ti + yi * tr], axis=1)
    data = right_product(split(data), (fh_ref[...], fl_ref[...]))
    data = data * jnp.concatenate([gain, gain], axis=1)
    data = right_product(split(data), (gh_ref[...], gl_ref[...]))
    yr, yi = data[:, :cols], data[:, cols:]
    data = jnp.concatenate([yr * tr + yi * ti, yi * tr - yr * ti], axis=1)
    parts = split(data)
    pr, pi = left_product(outer_r, parts), left_product(outer_i, parts)
    out_ref[pl.ds(0, rows, stride=2), :] = pr[:, :cols] + pi[:, cols:]
    out_ref[pl.ds(1, rows, stride=2), :] = pr[:, cols:] - pi[:, :cols]


HALO = 4


def edge_rows(value, xl, low_ref, high_ref, base):
    for layer in range(value.shape[0] // xl):
        at = base + layer * HALO
        low_ref[at : at + HALO] = value[layer * xl : layer * xl + HALO]
        high_ref[at : at + HALO] = value[(layer + 1) * xl - HALO : (layer + 1) * xl]


def widen(value_ref, low_ref, high_ref, base, xl, out_ref, fill=(0.0, 0.0)):
    for layer in range(value_ref.shape[0] // xl):
        to, at = layer * (xl + 2 * HALO), base + layer * HALO
        out_ref[to : to + xl] = value_ref[layer * xl : (layer + 1) * xl]
        out_ref[to + xl : to + xl + HALO] = high_ref[at : at + HALO] + fill[1]
        out_ref[to + xl + HALO : to + xl + 2 * HALO] = low_ref[at : at + HALO] + fill[0]


def field_kernel(xl, data_ref, th_ref, tl_ref, log_ref, q_ref, low_ref, high_ref):
    rows, half = th_ref.shape
    mid = rows // 2
    turned = jnp.transpose(data_ref[...])
    even = right_product(split(turned[:, :mid]), (th_ref[:mid], tl_ref[:mid]))
    odd = right_product(split(turned[:, mid:]), (th_ref[mid:], tl_ref[mid:]))
    log_ref[:, :half] = even + odd
    log_ref[:, half:] = even - odd
    q = 0.5 * jnp.exp(-log_ref[...])
    q_ref[...] = q
    edge_rows(q, xl, low_ref, high_ref, 0)


def widen_kernel(xl, edge_ref, q_ref, low_ref, high_ref, out_ref):
    widen(q_ref, low_ref, high_ref, 0, xl, out_ref, (1.0 - edge_ref[2], 1.0 - edge_ref[3]))


def rhs_kernel(xl, origin_ref, recharge_ref, cells_ref, rates_ref, storage_ref, rhs_ref, low_ref, high_ref):
    rows, length = recharge_ref.shape
    wells = cells_ref.shape[1]
    layer = cells_ref[0:1] - origin_ref[0]
    line = cells_ref[1:2] - origin_ref[1]
    inside = (line >= 0) & (line < xl)
    at = jnp.where(inside, layer * xl + line, -1)
    rate = jnp.where(lax.broadcasted_iota(jnp.int32, (rows, wells), 0) == at, rates_ref[...], 0.0)
    column = (lax.broadcasted_iota(jnp.int32, (length, wells), 0) == cells_ref[2:3]).astype(F32).astype(BF16)
    added = None
    for _ in range(3):
        part = rate.astype(BF16)
        rate = rate - part.astype(F32)
        product = lax.dot_general(part, column, (((1,), (1,)), ((), ())), preferred_element_type=F32)
        added = product if added is None else added + product
    rhs = recharge_ref[...] + added
    rhs_ref[...] = rhs
    edge_rows(storage_ref[...], xl, low_ref, high_ref, 0)
    edge_rows(rhs, xl, low_ref, high_ref, rows // xl * HALO)


def widen_pair_kernel(xl, storage_ref, rhs_ref, low_ref, high_ref, s_ref, r_ref, first_ref, last_ref):
    layers, wide = storage_ref.shape[0] // xl, xl + 2 * HALO
    widen(storage_ref, low_ref, high_ref, 0, xl, s_ref)
    widen(rhs_ref, low_ref, high_ref, layers * HALO, xl, r_ref)
    size = (layers - 1) * wide
    first_ref[:size] = s_ref[:size]
    first_ref[size:] = r_ref[:size]
    last_ref[:size] = s_ref[wide:]
    last_ref[size:] = r_ref[wide:]


def krylov_kernel(xl, edge_ref, q_ref, q_low, q_high, s_ref, r_ref, sr_low, sr_high, u0_out, u1_out, u2_out, u3_out, diag_out, mom_out, cz, cx, cy, inv, u0, u1, u2, u3, diag):
    wide, length = xl + 2 * HALO, q_ref.shape[1]
    own = q_ref.shape[0] // wide
    total = own + 2 * HALO
    z_lo, z_hi, x_lo, x_hi = (edge_ref[i] for i in range(4))
    row = lax.broadcasted_iota(jnp.int32, (wide, length), 0)
    lane = lax.broadcasted_iota(jnp.int32, (wide, length), 1)
    keep_x = jnp.where(row == xl - 1, x_hi, jnp.where(row == wide - 1, x_lo, 1.0))
    keep_y = jnp.where(lane == length - 1, 0.0, 1.0)

    def at(z):
        return pl.ds(z * wide, wide)

    def q_of(z):
        if z < HALO:
            return q_low[at(z)] + (1.0 - z_lo)
        if z >= HALO + own:
            return q_high[at(z - HALO - own)] + (1.0 - z_hi)
        return q_ref[at(z - HALO)]

    def pair_of(z):
        depth = own - 1
        if z < HALO:
            return sr_low[at(z - 1)], sr_low[at(depth + z - 1)]
        if z >= HALO + own:
            return sr_high[at(z - HALO - own)], sr_high[at(depth + z - HALO - own)]
        return s_ref[at(z - HALO)], r_ref[at(z - HALO)]

    def up_x(value):
        return pltpu.roll(value, wide - 1, 0)

    def down_x(value):
        return pltpu.roll(value, 1, 0)

    def up_y(value):
        return pltpu.roll(value, length - 1, 1)

    def down_y(value):
        return pltpu.roll(value, 1, 1)

    for z in range(total - 1):
        face = pl.reciprocal(q_of(z) + q_of(z + 1))
        if z == HALO - 1:
            face = face * z_lo
        if z == HALO + own - 1:
            face = face * z_hi
        cz[at(z)] = face
        if z == 0:
            continue
        q = q_of(z)
        storage, rhs = pair_of(z)
        face_x = pl.reciprocal(q + up_x(q)) * keep_x
        face_y = pl.reciprocal(q + up_y(q)) * keep_y
        cx[at(z)] = face_x
        cy[at(z)] = face_y
        d = storage + cz[at(z - 1)] + face + face_x + down_x(face_x) + face_y + down_y(face_y)
        inverse = pl.reciprocal(d)
        inv[at(z)] = inverse
        u0[at(z)] = rhs * inverse
        if HALO <= z < HALO + own:
            diag[pl.ds((z - HALO) * xl, xl)] = d[:xl]
    levels = (u0, u1, u2, u3)
    for level in range(3):
        old, new = levels[level], levels[level + 1]
        for z in range(2 + level, total - 2 - level):
            here, face_x, face_y = old[at(z)], cx[at(z)], cy[at(z)]
            flow = cz[at(z - 1)] * old[at(z - 1)] + cz[at(z)] * old[at(z + 1)]
            flow = flow + face_x * up_x(here) + down_x(face_x * here)
            flow = flow + face_y * up_y(here) + down_y(face_y * here)
            new[at(z)] = flow * inv[at(z)]
    sums = [None] * 6
    for z in range(HALO, HALO + own):
        to = pl.ds((z - HALO) * xl, xl)
        d = diag[to]
        values = [level[pl.ds(z * wide, xl)] for level in levels]
        for out, value in zip((u0_out, u1_out, u2_out, u3_out), values):
            out[to] = value
        diag_out[to] = d
        for i in range(6):
            if i % 2 == 0:
                weighted = d * values[i // 2]
            term = weighted * values[(i + 1) // 2]
            term = jnp.sum(term, axis=0, keepdims=True)
            sums[i] = term if sums[i] is None else sums[i] + term
    place = lax.broadcasted_iota(jnp.int32, (1, 128), 1)
    moments = jnp.zeros((1, 128), F32)
    for i in range(6):
        moments = jnp.where(place == i, jnp.sum(sums[i], axis=1, keepdims=True), moments)
    mom_out[...] = jnp.broadcast_to(moments, mom_out.shape)


def partial_kernel(in_ref, out_ref):
    out_ref[...] = jnp.broadcast_to(jnp.sum(in_ref[...], axis=0, keepdims=True), out_ref.shape)


def final_kernel(iters, mom_ref, u0, u1, u2, u3, diag_ref, pressure_ref, residual_ref):
    moments = jnp.sum(mom_ref[...], axis=0, keepdims=True)
    lane = lax.broadcasted_iota(jnp.int32, (1, 128), 1)
    nu = [jnp.sum(jnp.where(lane == i, moments, 0.0), axis=1, keepdims=True) for i in range(2 * iters)]

    def form(a, b):
        total = None
        for i, left in enumerate(a):
            for j, right in enumerate(b):
                term = left * right * nu[i + j]
                total = term if total is None else total + term
        return total

    one = jnp.ones((1, 1), F32)
    zero = jnp.zeros((1, 1), F32)
    precond, direction, pressure = [one], [one], [zero] * iters
    rz = nu[0]
    for it in range(iters):
        image = [
            (direction[i] if i < len(direction) else zero) - (direction[i - 1] if i > 0 else zero)
            for i in range(len(direction) + 1)
        ]
        alpha = rz / form(direction, image)
        pressure = [old + alpha * direction[i] if i < len(direction) else old for i, old in enumerate(pressure)]
        precond = [(precond[i] if i < len(precond) else zero) - alpha * image[i] for i in range(len(image))]
        if it + 1 < iters:
            new = form(precond, precond)
            beta = new / rz
            direction = [
                precond[i] + beta * direction[i] if i < len(direction) else precond[i] for i in range(len(precond))
            ]
            rz = new
    basis = [u0[...], u1[...], u2[...], u3[...]]
    pressure_ref[...] = pressure[0] * basis[0] + pressure[1] * basis[1] + pressure[2] * basis[2]
    total = precond[0] * basis[0] + precond[1] * basis[1] + precond[2] * basis[2] + precond[3] * basis[3]
    residual_ref[...] = diag_ref[...] * total


ITERS = 3


def exchange(low, high, axis):
    count = lax.axis_size(axis)
    up = [(i, i + 1) for i in range(count - 1)]
    down = [(i + 1, i) for i in range(count - 1)]
    return lax.ppermute(high, axis, up), lax.ppermute(low, axis, down)


def shards(seeds, lengths, exponents, storage, recharge, well_cells, well_rates):
    zl, xl, length_y = storage.shape
    gx, gy = lax.axis_size("gx"), lax.axis_size("gy")
    assert zl == HALO and xl >= HALO
    rows, wide = zl * xl, xl + 2 * HALO
    block, middle = f32(rows, length_y), f32(zl * wide, length_y)
    edge, edge_pair = f32(zl * HALO, length_y), f32(2 * zl * HALO, length_y)
    part = f32(2 * (zl - 1) * wide, length_y)
    at_x, at_y = lax.axis_index("gx"), lax.axis_index("gy")
    device = (at_x * gy + at_y).reshape(1).astype(jnp.int32)
    origin = jnp.stack([at_y * zl, at_x * xl]).astype(jnp.int32)
    edges = jnp.stack([at_y > 0, at_y < gy - 1, at_x > 0, at_x < gx - 1]).astype(F32)
    smem = pl.BlockSpec(memory_space=pltpu.SMEM)
    vmem = pl.BlockSpec(memory_space=pltpu.VMEM)
    ty = halves(table_y(length_y))
    outer, twiddle, inner = tables_zx(gx, gy, zl, xl)

    def everywhere(array):
        return lax.all_to_all(array, ("gx", "gy"), split_axis=0, concat_axis=0, tiled=True)

    flat_storage = storage.reshape(rows, length_y)
    rhs, low, high = call(
        lambda *refs: rhs_kernel(xl, *refs),
        [block, edge_pair, edge_pair],
        origin,
        recharge.reshape(rows, length_y),
        well_cells,
        well_rates.reshape(1, -1),
        flat_storage,
        specs=[smem] + [vmem] * 4,
    )
    low, high = exchange(low, high, "gx")
    wide_storage, wide_rhs, first, last = call(
        lambda *refs: widen_pair_kernel(xl, *refs), [middle, middle, part, part], flat_storage, rhs, low, high
    )
    pair_low, pair_high = exchange(first, last, "gy")

    spectrum = call(noise_kernel, f32(length_y, rows), seeds.reshape(1, rows), *ty)
    spectrum = everywhere(spectrum)
    spectrum = call(
        lambda *refs: spectrum_kernel((gx, gy, zl, xl, length_y), *refs),
        f32(length_y, rows),
        device,
        lengths,
        exponents,
        spectrum,
        *halves(outer.real),
        *halves(outer.imag),
        jnp.asarray(twiddle.real, F32),
        jnp.asarray(twiddle.imag, F32),
        *halves(inner),
        *halves(inner.T),
        specs=[smem, smem, smem] + [vmem] * 11,
    )
    spectrum = everywhere(spectrum)
    log_perm, q, low, high = call(
        lambda *refs: field_kernel(xl, *refs), [block, block, edge, edge], spectrum, *ty
    )
    low, high = exchange(low, high, "gx")
    q = call(lambda *refs: widen_kernel(xl, *refs), middle, edges, q, low, high, specs=[smem] + [vmem] * 3)
    q_low, q_high = exchange(q, q, "gy")

    layers = zl + 2 * HALO
    *basis, diag, moments = call(
        lambda *refs: krylov_kernel(xl, *refs),
        [block] * 5 + [f32(gx, 128)],
        edges,
        q,
        q_low,
        q_high,
        wide_storage,
        wide_rhs,
        pair_low,
        pair_high,
        specs=[smem] + [vmem] * 7,
        scratch=[pltpu.VMEM((layers * wide, length_y), F32)] * 8 + [pltpu.VMEM((rows, length_y), F32)],
    )
    moments = lax.all_to_all(moments, "gx", split_axis=0, concat_axis=0, tiled=True)
    moments = call(partial_kernel, f32(gy, 128), moments)
    moments = lax.all_to_all(moments, "gy", split_axis=0, concat_axis=0, tiled=True)
    pressure, residual = call(
        lambda *refs: final_kernel(ITERS, *refs), [block, block], moments, *basis, diag
    )
    shape = storage.shape
    return (log_perm.reshape(shape), pressure.reshape(shape), residual.reshape(shape))


def solution(mesh):
    placed = (P("gy", "gx"), P(), P(), P("gy", "gx", None), P("gy", "gx", None), P(), P())
    return jax.shard_map(
        shards,
        mesh=mesh,
        in_specs=placed,
        out_specs=(P("gy", "gx", None), P("gy", "gx", None), P("gy", "gx", None)),
        check_vma=False,
    )
```

```python
import math

import jax
import jax.numpy as jnp
import numpy as np
from jax import lax
from jax.experimental import pallas as pl
from jax.experimental.pallas import tpu as pltpu
from jax.sharding import PartitionSpec as P

AMPLITUDE = 4.0
BF16 = jnp.bfloat16
F32 = jnp.float32
INTERPRET = False


def call(body, outs, *args, specs=None, scratch=(), limit=60):
    return pl.pallas_call(
        body,
        out_shape=outs,
        in_specs=specs or [pl.BlockSpec(memory_space=pltpu.VMEM)] * len(args),
        scratch_shapes=scratch,
        interpret=INTERPRET,
        compiler_params=pltpu.CompilerParams(vmem_limit_bytes=limit * 2**20),
    )(*args)


def f32(*shape):
    return jax.ShapeDtypeStruct(shape, F32)


def on_chip(array):
    return array if INTERPRET else pltpu.with_memory_space_constraint(array, pltpu.MemorySpace.VMEM)


def halves(table):
    high = table.astype(BF16)
    low = (table - high.astype(np.float64)).astype(BF16)
    return jnp.asarray(high), jnp.asarray(low)


def cosine_sine(product, length):
    angle = (product % length).astype(np.float64) * (2.0 * math.pi / length)
    return np.cos(angle), np.sin(angle)


def table_y(length):
    half = length // 2
    k = np.concatenate([np.arange(0, half, 2), np.arange(1, half, 2)])
    cos, sin = cosine_sine(k[:, None] * np.arange(half)[None, :], length)
    return np.stack([cos, -sin], axis=1).reshape(2 * half, half)


def tables_zx(gx, gy, zl, xl):
    row_x, row_z = np.repeat(np.arange(gx), gy), np.tile(np.arange(gy), gx)
    col_x, col_z = np.tile(np.arange(xl), zl), np.repeat(np.arange(zl), xl)

    def table(left_x, right_x, left_z, right_z, size_x, size_z):
        phase = np.outer(left_x, right_x) / size_x + np.outer(left_z, right_z) / size_z
        return np.exp(-2j * math.pi * phase)

    outer = table(row_x, row_x, row_z, row_z, gx, gy)
    twiddle = table(row_x, col_x, row_z, col_z, gx * xl, gy * zl)
    inner = table(col_x, col_x, col_z, col_z, xl, zl)
    forward = np.block([[inner.real, inner.imag], [-inner.imag, inner.real]])
    return outer, twiddle, forward


def split(data):
    high = data.astype(BF16)
    return high, (data - high.astype(F32)).astype(BF16)


def dot(a, b):
    return jnp.dot(a, b, preferred_element_type=F32)


def left_product(table, data):
    (th, tl), (dh, dl) = table, data
    return dot(th, dh) + (dot(th, dl) + dot(tl, dh))


def right_product(data, table):
    (dh, dl), (th, tl) = data, table
    return dot(dh, th) + (dot(dl, th) + dot(dh, tl))


def mix_bits(seed_rows, cells):
    shift = lax.shift_right_logical
    hashed = seed_rows + cells * jnp.int32(-1640531535)
    hashed = hashed ^ shift(hashed, jnp.int32(16))
    hashed = hashed * jnp.int32(-2048144789)
    hashed = hashed ^ shift(hashed, jnp.int32(13))
    hashed = hashed * jnp.int32(-1028477387)
    hashed = hashed ^ shift(hashed, jnp.int32(16))
    value = shift(hashed, jnp.int32(8)).astype(F32)
    return (value + 0.5) * (2.0 * math.sqrt(3.0) / 16777216.0) - math.sqrt(3.0)


def noise_kernel(seed_ref, th_ref, tl_ref, out_ref):
    rows, half = th_ref.shape
    seeds = seed_ref[...]
    cells = lax.broadcasted_iota(jnp.int32, (half, seeds.shape[1]), 0)
    near = mix_bits(seeds, cells)
    far = mix_bits(seeds, cells + half)
    mid = rows // 2
    out_ref[:mid] = left_product((th_ref[:mid], tl_ref[:mid]), split(near + far))
    out_ref[mid:] = left_product((th_ref[mid:], tl_ref[mid:]), split(near - far))


def power(base, exponent):
    return jnp.exp(exponent * jnp.log(base))


def spectrum_kernel(sizes, device_ref, lengths_ref, exponents_ref, data_ref, ar_h, ar_l, ai_h, ai_l, tr_ref, ti_ref, fh_ref, fl_ref, gh_ref, gl_ref, *rest):
    out_ref = rest[-1]
    gx, gy, zl, xl, length_y = sizes
    rows, cols = gx * gy, zl * xl
    outer_r = (ar_h[...], ar_l[...])
    outer_i = (ai_h[...], ai_l[...])
    tr, ti = tr_ref[...], ti_ref[...]
    shape = (rows, cols)
    row = lax.broadcasted_iota(jnp.int32, shape, 0)
    col = lax.broadcasted_iota(jnp.int32, shape, 1)
    kx = lax.div(row, gy) + gx * lax.rem(col, xl)
    kz = lax.rem(row, gy) + gy * lax.div(col, xl)
    device = device_ref[0]
    half_rows = rows // 2
    ky = jnp.where(device < half_rows, 2 * device, 2 * (device - half_rows) + 1)

    def wave(index, length):
        folded = jnp.minimum(index, length - index)
        return folded.astype(F32) * (2.0 * math.pi / length)

    ky_all = jnp.full((8, cols), ky, jnp.int32)
    total_y = 1.0 + power(lengths_ref[2] * wave(ky_all, length_y), exponents_ref[2])
    weight = jnp.where(ky_all == 0, 1.0, 2.0)
    volume = jnp.full((8, cols), lengths_ref[0] * lengths_ref[1] * lengths_ref[2], F32)
    scale = 1.0 / (gx * xl * gy * zl * length_y)
    numerator = AMPLITUDE * jnp.sqrt(volume) * scale * weight
    total = power(lengths_ref[0] * wave(kz, gy * zl), exponents_ref[0])
    total = total + power(lengths_ref[1] * wave(kx, gx * xl), exponents_ref[1])
    gain = numerator[:1] / (total_y[:1] + total)
    data = jnp.concatenate([data_ref[pl.ds(0, rows, stride=2), :], data_ref[pl.ds(1, rows, stride=2), :]], axis=1)
    parts = split(data)
    pr, pi = left_product(outer_r, parts), left_product(outer_i, parts)
    yr, yi = pr[:, :cols] - pi[:, cols:], pr[:, cols:] + pi[:, :cols]
    data = jnp.concatenate([yr * tr - yi * ti, yr * ti + yi * tr], axis=1)
    data = right_product(split(data), (fh_ref[...], fl_ref[...]))
    data = data * jnp.concatenate([gain, gain], axis=1)
    data = right_product(split(data), (gh_ref[...], gl_ref[...]))
    yr, yi = data[:, :cols], data[:, cols:]
    data = jnp.concatenate([yr * tr + yi * ti, yi * tr - yr * ti], axis=1)
    parts = split(data)
    pr, pi = left_product(outer_r, parts), left_product(outer_i, parts)
    out_ref[pl.ds(0, rows, stride=2), :] = pr[:, :cols] + pi[:, cols:]
    out_ref[pl.ds(1, rows, stride=2), :] = pr[:, cols:] - pi[:, :cols]


HALO = 4


def edge_rows(value, xl, low_ref, high_ref, base):
    for layer in range(value.shape[0] // xl):
        at = base + layer * HALO
        low_ref[at : at + HALO] = value[layer * xl : layer * xl + HALO]
        high_ref[at : at + HALO] = value[(layer + 1) * xl - HALO : (layer + 1) * xl]


def field_kernel(xl, data_ref, th_ref, tl_ref, *refs):
    log_ref, q_ref, low_ref, high_ref = refs[-4:]
    rows, half = th_ref.shape
    mid = rows // 2
    turned = jnp.transpose(data_ref[...])
    even = right_product(split(turned[:, :mid]), (th_ref[:mid], tl_ref[:mid]))
    odd = right_product(split(turned[:, mid:]), (th_ref[mid:], tl_ref[mid:]))
    log_ref[:, :half] = even + odd
    log_ref[:, half:] = even - odd
    q = 0.5 * jnp.exp(-log_ref[...])
    q_ref[...] = q
    edge_rows(q, xl, low_ref, high_ref, 0)


def rhs_kernel(xl, origin_ref, recharge_ref, cells_ref, rates_ref, storage_ref, rhs_ref, first_ref, last_ref, low_ref, high_ref):
    rows, length = recharge_ref.shape
    wells = cells_ref.shape[1]
    layer = cells_ref[0:1] - origin_ref[0]
    line = cells_ref[1:2] - origin_ref[1]
    inside = (line >= 0) & (line < xl)
    at = jnp.where(inside, layer * xl + line, -1)
    rate = jnp.where(lax.broadcasted_iota(jnp.int32, (rows, wells), 0) == at, rates_ref[...], 0.0)
    column = (lax.broadcasted_iota(jnp.int32, (length, wells), 0) == cells_ref[2:3]).astype(F32).astype(BF16)
    added = None
    for _ in range(3):
        part = rate.astype(BF16)
        rate = rate - part.astype(F32)
        product = lax.dot_general(part, column, (((1,), (1,)), ((), ())), preferred_element_type=F32)
        added = product if added is None else added + product
    rhs = recharge_ref[...] + added
    rhs_ref[...] = rhs
    size = rows - xl
    first_ref[:size], first_ref[size:] = storage_ref[:size], rhs[:size]
    last_ref[:size], last_ref[size:] = storage_ref[xl:], rhs[xl:]
    edge_rows(storage_ref[...], xl, low_ref, high_ref, 0)
    edge_rows(rhs, xl, low_ref, high_ref, rows // xl * HALO)


def krylov_kernel(xl, edge_ref, *refs):
    q_ref, *q_halo = refs[:9]
    s_ref, r_ref, *pair_halo = refs[9:19]
    u0_out, u1_out, u2_out, u3_out, diag_out, mom_out = refs[19:25]
    q_all, s_all, r_all, cz, cx, cy, inv, u0, u1, u2, u3, diag = refs[25:]
    wide, length = xl + 2 * HALO, q_ref.shape[1]
    own = q_ref.shape[0] // xl
    total = own + 2 * HALO
    z_lo, z_hi, x_lo, x_hi = (edge_ref[i] for i in range(4))
    row = lax.broadcasted_iota(jnp.int32, (wide, length), 0)
    lane = lax.broadcasted_iota(jnp.int32, (wide, length), 1)
    keep_x = jnp.where(row == xl - 1, x_hi, jnp.where(row == wide - 1, x_lo, 1.0))
    keep_y = jnp.where(lane == length - 1, 0.0, 1.0)

    def at(z):
        return pl.ds(z * wide, wide)

    def place(out, z, value_ref, value_at, low_ref, high_ref, edge_at, fills):
        to = z * wide
        out[to : to + xl] = value_ref[value_at : value_at + xl] + fills[0]
        out[to + xl : to + xl + HALO] = high_ref[edge_at : edge_at + HALO] + fills[2]
        out[to + xl + HALO : to + wide] = low_ref[edge_at : edge_at + HALO] + fills[1]

    for side, (z_ok, corner) in enumerate(((z_lo, 4), (1.0, 2), (z_hi, 6))):
        fills = (1.0 - z_ok, 1.0 - z_ok * x_lo, 1.0 - z_ok * x_hi)
        low, high = q_halo[corner], q_halo[corner + 1]
        center = (q_halo[0], q_ref, q_halo[1])[side]
        for layer in range(own):
            place(q_all, side * HALO + layer, center, layer * xl, low, high, layer * HALO, fills)
        low, high = pair_halo[corner], pair_halo[corner + 1]
        skip = own - 1
        for part, out in enumerate((s_all, r_all)):
            for layer in ((1, 2, 3), (0, 1, 2, 3), (0, 1, 2))[side]:
                if side == 1:
                    center, value_at = (s_ref, r_ref)[part], layer * xl
                else:
                    center = pair_halo[side // 2]
                    value_at = (part * skip + layer - (1 if side == 0 else 0)) * xl
                edge_at = (part * own + layer) * HALO
                place(out, side * HALO + layer, center, value_at, low, high, edge_at, (0.0, 0.0, 0.0))

    def q_of(z):
        return q_all[at(z)]

    def up_x(value):
        return pltpu.roll(value, wide - 1, 0)

    def down_x(value):
        return pltpu.roll(value, 1, 0)

    def up_y(value):
        return pltpu.roll(value, length - 1, 1)

    def down_y(value):
        return pltpu.roll(value, 1, 1)

    for z in range(total - 1):
        face = pl.reciprocal(q_of(z) + q_of(z + 1))
        if z == HALO - 1:
            face = face * z_lo
        if z == HALO + own - 1:
            face = face * z_hi
        cz[at(z)] = face
        if z == 0:
            continue
        q = q_of(z)
        storage, rhs = s_all[at(z)], r_all[at(z)]
        face_x = pl.reciprocal(q + up_x(q)) * keep_x
        face_y = pl.reciprocal(q + up_y(q)) * keep_y
        cx[at(z)] = face_x
        cy[at(z)] = face_y
        d = storage + cz[at(z - 1)] + face + face_x + down_x(face_x) + face_y + down_y(face_y)
        inverse = pl.reciprocal(d)
        inv[at(z)] = inverse
        u0[at(z)] = rhs * inverse
        if HALO <= z < HALO + own:
            diag[pl.ds((z - HALO) * xl, xl)] = d[:xl]
    levels = (u0, u1, u2, u3)
    for level in range(3):
        old, new = levels[level], levels[level + 1]
        for z in range(2 + level, total - 2 - level):
            here, face_x, face_y = old[at(z)], cx[at(z)], cy[at(z)]
            flow = cz[at(z - 1)] * old[at(z - 1)] + cz[at(z)] * old[at(z + 1)]
            flow = flow + face_x * up_x(here) + down_x(face_x * here)
            flow = flow + face_y * up_y(here) + down_y(face_y * here)
            new[at(z)] = flow * inv[at(z)]
    sums = [None] * 6
    for z in range(HALO, HALO + own):
        to = pl.ds((z - HALO) * xl, xl)
        d = diag[to]
        values = [level[pl.ds(z * wide, xl)] for level in levels]
        for out, value in zip((u0_out, u1_out, u2_out, u3_out), values):
            out[to] = value
        diag_out[to] = d
        for i in range(6):
            if i % 2 == 0:
                weighted = d * values[i // 2]
            term = weighted * values[(i + 1) // 2]
            term = jnp.sum(term, axis=0, keepdims=True)
            sums[i] = term if sums[i] is None else sums[i] + term
    place = lax.broadcasted_iota(jnp.int32, (1, 128), 1)
    moments = jnp.zeros((1, 128), F32)
    for i in range(6):
        moments = jnp.where(place == i, jnp.sum(sums[i], axis=1, keepdims=True), moments)
    mom_out[...] = jnp.broadcast_to(moments, mom_out.shape)


def partial_kernel(in_ref, out_ref):
    out_ref[...] = jnp.broadcast_to(jnp.sum(in_ref[...], axis=0, keepdims=True), out_ref.shape)


def final_kernel(iters, mom_ref, u0, u1, u2, u3, diag_ref, pressure_ref, residual_ref):
    moments = jnp.sum(mom_ref[...], axis=0, keepdims=True)
    lane = lax.broadcasted_iota(jnp.int32, (1, 128), 1)
    nu = [jnp.sum(jnp.where(lane == i, moments, 0.0), axis=1, keepdims=True) for i in range(2 * iters)]

    def form(a, b):
        total = None
        for i, left in enumerate(a):
            for j, right in enumerate(b):
                term = left * right * nu[i + j]
                total = term if total is None else total + term
        return total

    one = jnp.ones((1, 1), F32)
    zero = jnp.zeros((1, 1), F32)
    precond, direction, pressure = [one], [one], [zero] * iters
    rz = nu[0]
    for it in range(iters):
        image = [
            (direction[i] if i < len(direction) else zero) - (direction[i - 1] if i > 0 else zero)
            for i in range(len(direction) + 1)
        ]
        alpha = rz / form(direction, image)
        pressure = [old + alpha * direction[i] if i < len(direction) else old for i, old in enumerate(pressure)]
        precond = [(precond[i] if i < len(precond) else zero) - alpha * image[i] for i in range(len(image))]
        if it + 1 < iters:
            new = form(precond, precond)
            beta = new / rz
            direction = [
                precond[i] + beta * direction[i] if i < len(direction) else precond[i] for i in range(len(precond))
            ]
            rz = new
    basis = [u0[...], u1[...], u2[...], u3[...]]
    pressure_ref[...] = pressure[0] * basis[0] + pressure[1] * basis[1] + pressure[2] * basis[2]
    total = precond[0] * basis[0] + precond[1] * basis[1] + precond[2] * basis[2] + precond[3] * basis[3]
    residual_ref[...] = diag_ref[...] * total


ITERS = 3


def halo_exchange(first, last, low, high):
    gx, gy = lax.axis_size("gx"), lax.axis_size("gy")

    def move(array, step_x, step_y):
        pairs = [
            (i * gy + j, (i + step_x) * gy + j + step_y)
            for i in range(gx)
            for j in range(gy)
            if 0 <= i + step_x < gx and 0 <= j + step_y < gy
        ]
        return lax.ppermute(array, ("gx", "gy"), pairs)

    return [
        move(last, 0, 1),
        move(first, 0, -1),
        move(high, 1, 0),
        move(low, -1, 0),
        move(high, 1, 1),
        move(low, -1, 1),
        move(high, 1, -1),
        move(low, -1, -1),
    ]


def shards(seeds, lengths, exponents, storage, recharge, well_cells, well_rates):
    zl, xl, length_y = storage.shape
    gx, gy = lax.axis_size("gx"), lax.axis_size("gy")
    assert zl == HALO and xl >= HALO
    rows, wide = zl * xl, xl + 2 * HALO
    block, part = f32(rows, length_y), f32(2 * (rows - xl), length_y)
    edge, edge_pair = f32(zl * HALO, length_y), f32(2 * zl * HALO, length_y)
    at_x, at_y = lax.axis_index("gx"), lax.axis_index("gy")
    device = (at_x * gy + at_y).reshape(1).astype(jnp.int32)
    origin = jnp.stack([at_y * zl, at_x * xl]).astype(jnp.int32)
    edges = jnp.stack([at_y > 0, at_y < gy - 1, at_x > 0, at_x < gx - 1]).astype(F32)
    smem = pl.BlockSpec(memory_space=pltpu.SMEM)
    vmem = pl.BlockSpec(memory_space=pltpu.VMEM)
    ty = halves(table_y(length_y))
    outer, twiddle, inner = tables_zx(gx, gy, zl, xl)
    tables = [*halves(outer.real), *halves(outer.imag), jnp.asarray(twiddle.real, F32), jnp.asarray(twiddle.imag, F32)]
    tables += [*halves(inner), *halves(inner.T)]

    def everywhere(array):
        return on_chip(lax.all_to_all(array, ("gx", "gy"), split_axis=0, concat_axis=0, tiled=True))

    flat_storage = storage.reshape(rows, length_y)
    rhs, *sides = call(
        lambda *refs: rhs_kernel(xl, *refs),
        [block, part, part, edge_pair, edge_pair],
        origin,
        recharge.reshape(rows, length_y),
        well_cells,
        well_rates.reshape(1, -1),
        flat_storage,
        specs=[smem] + [vmem] * 4,
    )
    pair_halo = halo_exchange(*sides)

    spectrum = call(noise_kernel, f32(length_y, rows), seeds.reshape(1, rows), *ty)
    spectrum = everywhere(spectrum)
    spectrum = call(
        lambda *refs: spectrum_kernel((gx, gy, zl, xl, length_y), *refs),
        f32(length_y, rows),
        device,
        lengths,
        exponents,
        spectrum,
        *tables,
        *pair_halo[:4],
        specs=[smem, smem, smem] + [vmem] * 11 + [pl.BlockSpec(memory_space=pl.ANY)] * 4,
    )
    spectrum = everywhere(spectrum)
    log_perm, q, low, high = call(
        lambda *refs: field_kernel(xl, *refs),
        [block, block, edge, edge],
        spectrum,
        *ty,
        *pair_halo[4:],
        specs=[vmem] * 3 + [pl.BlockSpec(memory_space=pl.ANY)] * 4,
    )
    q_halo = [on_chip(side) for side in halo_exchange(q, q, low, high)]

    layers = zl + 2 * HALO
    *basis, diag, moments = call(
        lambda *refs: krylov_kernel(xl, *refs),
        [block] * 5 + [f32(gx, 128)],
        edges,
        q,
        *q_halo,
        flat_storage,
        rhs,
        *pair_halo,
        specs=[smem] + [vmem] * 19,
        scratch=[pltpu.VMEM((layers * wide, length_y), F32)] * 11 + [pltpu.VMEM((rows, length_y), F32)],
        limit=60,
    )
    moments = lax.all_to_all(moments, "gx", split_axis=0, concat_axis=0, tiled=True)
    moments = call(partial_kernel, f32(gy, 128), moments)
    moments = lax.all_to_all(moments, "gy", split_axis=0, concat_axis=0, tiled=True)
    pressure, residual = call(
        lambda *refs: final_kernel(ITERS, *refs), [block, block], moments, *basis, diag
    )
    shape = storage.shape
    return (log_perm.reshape(shape), pressure.reshape(shape), residual.reshape(shape))


def solution(mesh):
    placed = (P("gy", "gx"), P(), P(), P("gy", "gx", None), P("gy", "gx", None), P(), P())
    return jax.shard_map(
        shards,
        mesh=mesh,
        in_specs=placed,
        out_specs=(P("gy", "gx", None), P("gy", "gx", None), P("gy", "gx", None)),
        check_vma=False,
    )
```

```python
import math

import jax
import jax.numpy as jnp
import numpy as np
from jax import lax
from jax.experimental import pallas as pl
from jax.experimental.pallas import tpu as pltpu
from jax.sharding import PartitionSpec as P

AMPLITUDE = 4.0
BF16 = jnp.bfloat16
F32 = jnp.float32
INTERPRET = False


def call(body, outs, *args, specs=None, scratch=(), limit=60):
    return pl.pallas_call(
        body,
        out_shape=outs,
        in_specs=specs or [pl.BlockSpec(memory_space=pltpu.VMEM)] * len(args),
        scratch_shapes=scratch,
        interpret=INTERPRET,
        compiler_params=pltpu.CompilerParams(vmem_limit_bytes=limit * 2**20),
    )(*args)


def f32(*shape):
    return jax.ShapeDtypeStruct(shape, F32)


def on_chip(array):
    return array if INTERPRET else pltpu.with_memory_space_constraint(array, pltpu.MemorySpace.VMEM)


def halves(table):
    high = table.astype(BF16)
    low = (table - high.astype(np.float64)).astype(BF16)
    return jnp.asarray(high), jnp.asarray(low)


def cosine_sine(product, length):
    angle = (product % length).astype(np.float64) * (2.0 * math.pi / length)
    return np.cos(angle), np.sin(angle)


def table_y(length):
    half = length // 2
    k = np.concatenate([np.arange(0, half, 2), np.arange(1, half, 2)])
    cos, sin = cosine_sine(k[:, None] * np.arange(half)[None, :], length)
    return np.stack([cos, -sin], axis=1).reshape(2 * half, half)


def tables_zx(gx, gy, zl, xl):
    row_x, row_z = np.repeat(np.arange(gx), gy), np.tile(np.arange(gy), gx)
    col_x, col_z = np.tile(np.arange(xl), zl), np.repeat(np.arange(zl), xl)

    def table(left_x, right_x, left_z, right_z, size_x, size_z):
        phase = np.outer(left_x, right_x) / size_x + np.outer(left_z, right_z) / size_z
        return np.exp(-2j * math.pi * phase)

    outer = table(row_x, row_x, row_z, row_z, gx, gy)
    twiddle = table(row_x, col_x, row_z, col_z, gx * xl, gy * zl)
    inner = table(col_x, col_x, col_z, col_z, xl, zl)
    forward = np.block([[inner.real, inner.imag], [-inner.imag, inner.real]])
    return outer, twiddle, forward


def split(data):
    high = data.astype(BF16)
    return high, (data - high.astype(F32)).astype(BF16)


def dot(a, b):
    return jnp.dot(a, b, preferred_element_type=F32)


def left_product(table, data):
    (th, tl), (dh, dl) = table, data
    return dot(th, dh) + (dot(th, dl) + dot(tl, dh))


def right_product(data, table):
    (dh, dl), (th, tl) = data, table
    return dot(dh, th) + (dot(dl, th) + dot(dh, tl))


def mix_bits(seed_rows, cells):
    shift = lax.shift_right_logical
    hashed = seed_rows + cells * jnp.int32(-1640531535)
    hashed = hashed ^ shift(hashed, jnp.int32(16))
    hashed = hashed * jnp.int32(-2048144789)
    hashed = hashed ^ shift(hashed, jnp.int32(13))
    hashed = hashed * jnp.int32(-1028477387)
    hashed = hashed ^ shift(hashed, jnp.int32(16))
    value = shift(hashed, jnp.int32(8)).astype(F32)
    return (value + 0.5) * (2.0 * math.sqrt(3.0) / 16777216.0) - math.sqrt(3.0)


def noise_kernel(seed_ref, th_ref, tl_ref, out_ref):
    rows, half = th_ref.shape
    seeds = seed_ref[...]
    cells = lax.broadcasted_iota(jnp.int32, (half, seeds.shape[1]), 0)
    near = mix_bits(seeds, cells)
    far = mix_bits(seeds, cells + half)
    mid = rows // 2
    out_ref[:mid] = left_product((th_ref[:mid], tl_ref[:mid]), split(near + far))
    out_ref[mid:] = left_product((th_ref[mid:], tl_ref[mid:]), split(near - far))


def power(base, exponent):
    return jnp.exp(exponent * jnp.log(base))


def spectrum_kernel(sizes, device_ref, lengths_ref, exponents_ref, data_ref, ar_h, ar_l, ai_h, ai_l, tr_ref, ti_ref, fh_ref, fl_ref, gh_ref, gl_ref, *rest):
    out_ref = rest[-1]
    gx, gy, zl, xl, length_y = sizes
    rows, cols = gx * gy, zl * xl
    outer_r = (ar_h[...], ar_l[...])
    outer_i = (ai_h[...], ai_l[...])
    tr, ti = tr_ref[...], ti_ref[...]
    shape = (rows, cols)
    row = lax.broadcasted_iota(jnp.int32, shape, 0)
    col = lax.broadcasted_iota(jnp.int32, shape, 1)
    kx = lax.div(row, gy) + gx * lax.rem(col, xl)
    kz = lax.rem(row, gy) + gy * lax.div(col, xl)
    device = device_ref[0]
    half_rows = rows // 2
    ky = jnp.where(device < half_rows, 2 * device, 2 * (device - half_rows) + 1)

    def wave(index, length):
        folded = jnp.minimum(index, length - index)
        return folded.astype(F32) * (2.0 * math.pi / length)

    ky_all = jnp.full((8, cols), ky, jnp.int32)
    total_y = 1.0 + power(lengths_ref[2] * wave(ky_all, length_y), exponents_ref[2])
    weight = jnp.where(ky_all == 0, 1.0, 2.0)
    volume = jnp.full((8, cols), lengths_ref[0] * lengths_ref[1] * lengths_ref[2], F32)
    scale = 1.0 / (gx * xl * gy * zl * length_y)
    numerator = AMPLITUDE * jnp.sqrt(volume) * scale * weight
    total = power(lengths_ref[0] * wave(kz, gy * zl), exponents_ref[0])
    total = total + power(lengths_ref[1] * wave(kx, gx * xl), exponents_ref[1])
    gain = numerator[:1] / (total_y[:1] + total)
    data = jnp.concatenate([data_ref[pl.ds(0, rows, stride=2), :], data_ref[pl.ds(1, rows, stride=2), :]], axis=1)
    parts = split(data)
    pr, pi = left_product(outer_r, parts), left_product(outer_i, parts)
    yr, yi = pr[:, :cols] - pi[:, cols:], pr[:, cols:] + pi[:, :cols]
    data = jnp.concatenate([yr * tr - yi * ti, yr * ti + yi * tr], axis=1)
    data = right_product(split(data), (fh_ref[...], fl_ref[...]))
    data = data * jnp.concatenate([gain, gain], axis=1)
    data = right_product(split(data), (gh_ref[...], gl_ref[...]))
    yr, yi = data[:, :cols], data[:, cols:]
    data = jnp.concatenate([yr * tr + yi * ti, yi * tr - yr * ti], axis=1)
    parts = split(data)
    pr, pi = left_product(outer_r, parts), left_product(outer_i, parts)
    out_ref[pl.ds(0, rows, stride=2), :] = pr[:, :cols] + pi[:, cols:]
    out_ref[pl.ds(1, rows, stride=2), :] = pr[:, cols:] - pi[:, :cols]


HALO = 4


def edge_rows(value, xl, low_ref, high_ref, base):
    for layer in range(value.shape[0] // xl):
        at = base + layer * HALO
        low_ref[at : at + HALO] = value[layer * xl : layer * xl + HALO]
        high_ref[at : at + HALO] = value[(layer + 1) * xl - HALO : (layer + 1) * xl]


def widen(value_ref, low_ref, high_ref, base, xl, out_ref):
    for layer in range(value_ref.shape[0] // xl):
        to, at = layer * (xl + 2 * HALO), base + layer * HALO
        out_ref[to : to + xl] = value_ref[layer * xl : (layer + 1) * xl]
        out_ref[to + xl : to + xl + HALO] = high_ref[at : at + HALO]
        out_ref[to + xl + HALO : to + xl + 2 * HALO] = low_ref[at : at + HALO]


def field_kernel(xl, data_ref, th_ref, tl_ref, *refs):
    log_ref, q_ref, low_ref, high_ref = refs[-4:]
    rows, half = th_ref.shape
    mid = rows // 2
    turned = jnp.transpose(data_ref[...])
    even = right_product(split(turned[:, :mid]), (th_ref[:mid], tl_ref[:mid]))
    odd = right_product(split(turned[:, mid:]), (th_ref[mid:], tl_ref[mid:]))
    log_ref[:, :half] = even + odd
    log_ref[:, half:] = even - odd
    q = 0.5 * jnp.exp(-log_ref[...])
    q_ref[...] = q
    edge_rows(q, xl, low_ref, high_ref, 0)


def rhs_kernel(xl, origin_ref, recharge_ref, cells_ref, rates_ref, storage_ref, rhs_ref, low_ref, high_ref):
    rows, length = recharge_ref.shape
    wells = cells_ref.shape[1]
    layer = cells_ref[0:1] - origin_ref[0]
    line = cells_ref[1:2] - origin_ref[1]
    inside = (line >= 0) & (line < xl)
    at = jnp.where(inside, layer * xl + line, -1)
    rate = jnp.where(lax.broadcasted_iota(jnp.int32, (rows, wells), 0) == at, rates_ref[...], 0.0)
    column = (lax.broadcasted_iota(jnp.int32, (length, wells), 0) == cells_ref[2:3]).astype(F32).astype(BF16)
    added = None
    for _ in range(3):
        part = rate.astype(BF16)
        rate = rate - part.astype(F32)
        product = lax.dot_general(part, column, (((1,), (1,)), ((), ())), preferred_element_type=F32)
        added = product if added is None else added + product
    rhs = recharge_ref[...] + added
    rhs_ref[...] = rhs
    edge_rows(storage_ref[...], xl, low_ref, high_ref, 0)
    edge_rows(rhs, xl, low_ref, high_ref, rows // xl * HALO)


def widen_pair_kernel(xl, storage_ref, rhs_ref, low_ref, high_ref, s_ref, r_ref, first_ref, last_ref):
    layers, wide = storage_ref.shape[0] // xl, xl + 2 * HALO
    widen(storage_ref, low_ref, high_ref, 0, xl, s_ref)
    widen(rhs_ref, low_ref, high_ref, layers * HALO, xl, r_ref)
    size = (layers - 1) * wide
    first_ref[:size] = s_ref[:size]
    first_ref[size:] = r_ref[:size]
    last_ref[:size] = s_ref[wide:]
    last_ref[size:] = r_ref[wide:]


def krylov_kernel(xl, edge_ref, *refs):
    q_ref, *q_halo = refs[:9]
    s_ref, r_ref, sr_low, sr_high = refs[9:13]
    u0_out, u1_out, u2_out, u3_out, diag_out, mom_out = refs[13:19]
    q_all, cz, cx, cy, inv, u0, u1, u2, u3, diag = refs[19:]
    wide, length = xl + 2 * HALO, q_ref.shape[1]
    own = q_ref.shape[0] // xl
    total = own + 2 * HALO
    z_lo, z_hi, x_lo, x_hi = (edge_ref[i] for i in range(4))
    row = lax.broadcasted_iota(jnp.int32, (wide, length), 0)
    lane = lax.broadcasted_iota(jnp.int32, (wide, length), 1)
    keep_x = jnp.where(row == xl - 1, x_hi, jnp.where(row == wide - 1, x_lo, 1.0))
    keep_y = jnp.where(lane == length - 1, 0.0, 1.0)

    def at(z):
        return pl.ds(z * wide, wide)

    def place(out, z, value_ref, value_at, low_ref, high_ref, edge_at, fills):
        to = z * wide
        out[to : to + xl] = value_ref[value_at : value_at + xl] + fills[0]
        out[to + xl : to + xl + HALO] = high_ref[edge_at : edge_at + HALO] + fills[2]
        out[to + xl + HALO : to + wide] = low_ref[edge_at : edge_at + HALO] + fills[1]

    for side, (z_ok, corner) in enumerate(((z_lo, 4), (1.0, 2), (z_hi, 6))):
        fills = (1.0 - z_ok, 1.0 - z_ok * x_lo, 1.0 - z_ok * x_hi)
        low, high = q_halo[corner], q_halo[corner + 1]
        center = (q_halo[0], q_ref, q_halo[1])[side]
        for layer in range(own):
            place(q_all, side * HALO + layer, center, layer * xl, low, high, layer * HALO, fills)

    def q_of(z):
        return q_all[at(z)]

    def pair_of(z):
        depth = own - 1
        if z < HALO:
            return sr_low[at(z - 1)], sr_low[at(depth + z - 1)]
        if z >= HALO + own:
            return sr_high[at(z - HALO - own)], sr_high[at(depth + z - HALO - own)]
        return s_ref[at(z - HALO)], r_ref[at(z - HALO)]

    def up_x(value):
        return pltpu.roll(value, wide - 1, 0)

    def down_x(value):
        return pltpu.roll(value, 1, 0)

    def up_y(value):
        return pltpu.roll(value, length - 1, 1)

    def down_y(value):
        return pltpu.roll(value, 1, 1)

    for z in range(total - 1):
        face = pl.reciprocal(q_of(z) + q_of(z + 1))
        if z == HALO - 1:
            face = face * z_lo
        if z == HALO + own - 1:
            face = face * z_hi
        cz[at(z)] = face
        if z == 0:
            continue
        q = q_of(z)
        storage, rhs = pair_of(z)
        face_x = pl.reciprocal(q + up_x(q)) * keep_x
        face_y = pl.reciprocal(q + up_y(q)) * keep_y
        cx[at(z)] = face_x
        cy[at(z)] = face_y
        d = storage + cz[at(z - 1)] + face + face_x + down_x(face_x) + face_y + down_y(face_y)
        inverse = pl.reciprocal(d)
        inv[at(z)] = inverse
        u0[at(z)] = rhs * inverse
        if HALO <= z < HALO + own:
            diag[pl.ds((z - HALO) * xl, xl)] = d[:xl]
    levels = (u0, u1, u2, u3)
    for level in range(3):
        old, new = levels[level], levels[level + 1]
        for z in range(2 + level, total - 2 - level):
            here, face_x, face_y = old[at(z)], cx[at(z)], cy[at(z)]
            flow = cz[at(z - 1)] * old[at(z - 1)] + cz[at(z)] * old[at(z + 1)]
            flow = flow + face_x * up_x(here) + down_x(face_x * here)
            flow = flow + face_y * up_y(here) + down_y(face_y * here)
            new[at(z)] = flow * inv[at(z)]
    sums = [None] * 6
    for z in range(HALO, HALO + own):
        to = pl.ds((z - HALO) * xl, xl)
        d = diag[to]
        values = [level[pl.ds(z * wide, xl)] for level in levels]
        for out, value in zip((u0_out, u1_out, u2_out, u3_out), values):
            out[to] = value
        diag_out[to] = d
        for i in range(6):
            if i % 2 == 0:
                weighted = d * values[i // 2]
            term = weighted * values[(i + 1) // 2]
            term = jnp.sum(term, axis=0, keepdims=True)
            sums[i] = term if sums[i] is None else sums[i] + term
    place = lax.broadcasted_iota(jnp.int32, (1, 128), 1)
    moments = jnp.zeros((1, 128), F32)
    for i in range(6):
        moments = jnp.where(place == i, jnp.sum(sums[i], axis=1, keepdims=True), moments)
    mom_out[...] = jnp.broadcast_to(moments, mom_out.shape)


def partial_kernel(in_ref, out_ref):
    out_ref[...] = jnp.broadcast_to(jnp.sum(in_ref[...], axis=0, keepdims=True), out_ref.shape)


def final_kernel(iters, mom_ref, u0, u1, u2, u3, diag_ref, pressure_ref, residual_ref):
    moments = jnp.sum(mom_ref[...], axis=0, keepdims=True)
    lane = lax.broadcasted_iota(jnp.int32, (1, 128), 1)
    nu = [jnp.sum(jnp.where(lane == i, moments, 0.0), axis=1, keepdims=True) for i in range(2 * iters)]

    def form(a, b):
        total = None
        for i, left in enumerate(a):
            for j, right in enumerate(b):
                term = left * right * nu[i + j]
                total = term if total is None else total + term
        return total

    one = jnp.ones((1, 1), F32)
    zero = jnp.zeros((1, 1), F32)
    precond, direction, pressure = [one], [one], [zero] * iters
    rz = nu[0]
    for it in range(iters):
        image = [
            (direction[i] if i < len(direction) else zero) - (direction[i - 1] if i > 0 else zero)
            for i in range(len(direction) + 1)
        ]
        alpha = rz / form(direction, image)
        pressure = [old + alpha * direction[i] if i < len(direction) else old for i, old in enumerate(pressure)]
        precond = [(precond[i] if i < len(precond) else zero) - alpha * image[i] for i in range(len(image))]
        if it + 1 < iters:
            new = form(precond, precond)
            beta = new / rz
            direction = [
                precond[i] + beta * direction[i] if i < len(direction) else precond[i] for i in range(len(precond))
            ]
            rz = new
    basis = [u0[...], u1[...], u2[...], u3[...]]
    pressure_ref[...] = pressure[0] * basis[0] + pressure[1] * basis[1] + pressure[2] * basis[2]
    total = precond[0] * basis[0] + precond[1] * basis[1] + precond[2] * basis[2] + precond[3] * basis[3]
    residual_ref[...] = diag_ref[...] * total


ITERS = 3


def exchange(low, high, axis):
    count = lax.axis_size(axis)
    up = [(i, i + 1) for i in range(count - 1)]
    down = [(i + 1, i) for i in range(count - 1)]
    return lax.ppermute(high, axis, up), lax.ppermute(low, axis, down)


def halo_exchange(first, last, low, high):
    gx, gy = lax.axis_size("gx"), lax.axis_size("gy")

    def move(array, step_x, step_y):
        pairs = [
            (i * gy + j, (i + step_x) * gy + j + step_y)
            for i in range(gx)
            for j in range(gy)
            if 0 <= i + step_x < gx and 0 <= j + step_y < gy
        ]
        return lax.ppermute(array, ("gx", "gy"), pairs)

    return [
        move(last, 0, 1),
        move(first, 0, -1),
        move(high, 1, 0),
        move(low, -1, 0),
        move(high, 1, 1),
        move(low, -1, 1),
        move(high, 1, -1),
        move(low, -1, -1),
    ]


def shards(seeds, lengths, exponents, storage, recharge, well_cells, well_rates):
    zl, xl, length_y = storage.shape
    gx, gy = lax.axis_size("gx"), lax.axis_size("gy")
    assert zl == HALO and xl >= HALO
    rows, wide = zl * xl, xl + 2 * HALO
    block, middle, part = f32(rows, length_y), f32(zl * wide, length_y), f32(2 * (zl - 1) * wide, length_y)
    edge, edge_pair = f32(zl * HALO, length_y), f32(2 * zl * HALO, length_y)
    at_x, at_y = lax.axis_index("gx"), lax.axis_index("gy")
    device = (at_x * gy + at_y).reshape(1).astype(jnp.int32)
    origin = jnp.stack([at_y * zl, at_x * xl]).astype(jnp.int32)
    edges = jnp.stack([at_y > 0, at_y < gy - 1, at_x > 0, at_x < gx - 1]).astype(F32)
    smem = pl.BlockSpec(memory_space=pltpu.SMEM)
    vmem = pl.BlockSpec(memory_space=pltpu.VMEM)
    ty = halves(table_y(length_y))
    outer, twiddle, inner = tables_zx(gx, gy, zl, xl)
    tables = [*halves(outer.real), *halves(outer.imag), jnp.asarray(twiddle.real, F32), jnp.asarray(twiddle.imag, F32)]
    tables += [*halves(inner), *halves(inner.T)]

    def everywhere(array):
        return on_chip(lax.all_to_all(array, ("gx", "gy"), split_axis=0, concat_axis=0, tiled=True))

    flat_storage = storage.reshape(rows, length_y)
    rhs, low, high = call(
        lambda *refs: rhs_kernel(xl, *refs),
        [block, edge_pair, edge_pair],
        origin,
        recharge.reshape(rows, length_y),
        well_cells,
        well_rates.reshape(1, -1),
        flat_storage,
        specs=[smem] + [vmem] * 4,
    )
    pair_x = exchange(low, high, "gx")
    wide_storage, wide_rhs, first, last = call(
        lambda *refs: widen_pair_kernel(xl, *refs), [middle, middle, part, part], flat_storage, rhs, *pair_x
    )
    pair_low, pair_high = exchange(first, last, "gy")

    spectrum = call(noise_kernel, f32(length_y, rows), seeds.reshape(1, rows), *ty)
    spectrum = everywhere(spectrum)
    spectrum = call(
        lambda *refs: spectrum_kernel((gx, gy, zl, xl, length_y), *refs),
        f32(length_y, rows),
        device,
        lengths,
        exponents,
        spectrum,
        *tables,
        *pair_x,
        specs=[smem, smem, smem] + [vmem] * 11 + [pl.BlockSpec(memory_space=pl.ANY)] * 2,
    )
    spectrum = everywhere(spectrum)
    log_perm, q, low, high = call(
        lambda *refs: field_kernel(xl, *refs),
        [block, block, edge, edge],
        spectrum,
        *ty,
        first,
        specs=[vmem] * 3 + [pl.BlockSpec(memory_space=pl.ANY)],
    )
    q_halo = [on_chip(side) for side in halo_exchange(q, q, low, high)]

    layers = zl + 2 * HALO
    *basis, diag, moments = call(
        lambda *refs: krylov_kernel(xl, *refs),
        [block] * 5 + [f32(gx, 128)],
        edges,
        q,
        *q_halo,
        wide_storage,
        wide_rhs,
        pair_low,
        pair_high,
        specs=[smem] + [vmem] * 13,
        scratch=[pltpu.VMEM((layers * wide, length_y), F32)] * 9 + [pltpu.VMEM((rows, length_y), F32)],
        limit=60,
    )
    moments = lax.all_to_all(moments, "gx", split_axis=0, concat_axis=0, tiled=True)
    moments = call(partial_kernel, f32(gy, 128), moments)
    moments = lax.all_to_all(moments, "gy", split_axis=0, concat_axis=0, tiled=True)
    pressure, residual = call(
        lambda *refs: final_kernel(ITERS, *refs), [block, block], moments, *basis, diag
    )
    shape = storage.shape
    return (log_perm.reshape(shape), pressure.reshape(shape), residual.reshape(shape))


def solution(mesh):
    placed = (P("gy", "gx"), P(), P(), P("gy", "gx", None), P("gy", "gx", None), P(), P())
    return jax.shard_map(
        shards,
        mesh=mesh,
        in_specs=placed,
        out_specs=(P("gy", "gx", None), P("gy", "gx", None), P("gy", "gx", None)),
        check_vma=False,
    )
```

```python
import math

import jax
import jax.numpy as jnp
import numpy as np
from jax import lax
from jax.experimental import pallas as pl
from jax.experimental.pallas import tpu as pltpu
from jax.sharding import PartitionSpec as P

AMPLITUDE = 4.0
BF16 = jnp.bfloat16
F32 = jnp.float32
INTERPRET = False
HALO = 4


def call(body, outs, *args, specs=None, scratch=(), limit=60):
    return pl.pallas_call(
        body,
        out_shape=outs,
        in_specs=specs or [pl.BlockSpec(memory_space=pltpu.VMEM)] * len(args),
        scratch_shapes=scratch,
        interpret=INTERPRET,
        compiler_params=pltpu.CompilerParams(vmem_limit_bytes=limit * 2**20),
    )(*args)


def f32(*shape):
    return jax.ShapeDtypeStruct(shape, F32)


def on_chip(array):
    return array if INTERPRET else pltpu.with_memory_space_constraint(array, pltpu.MemorySpace.VMEM)


def halves(table):
    high = table.astype(BF16)
    low = (table - high.astype(np.float64)).astype(BF16)
    return jnp.asarray(high), jnp.asarray(low)


def cosine_sine(product, length):
    angle = (product % length).astype(np.float64) * (2.0 * math.pi / length)
    return np.cos(angle), np.sin(angle)


def table_y(length):
    half = length // 2
    k = np.arange(half).reshape(half // 2, 2).T
    cos, sin = cosine_sine(k[:, :, None] * np.arange(half), length)
    return np.stack([cos, -sin], axis=1).reshape(2 * half, half)


def tables_zx(gx, gy, zl, xl):
    row_x, row_z = np.repeat(np.arange(gx), gy), np.tile(np.arange(gy), gx)
    col_x, col_z = np.tile(np.arange(xl), zl), np.repeat(np.arange(zl), xl)

    def table(left_x, right_x, left_z, right_z, size_x, size_z):
        phase = np.outer(left_x, right_x) / size_x + np.outer(left_z, right_z) / size_z
        return np.exp(-2j * math.pi * phase)

    outer = table(row_x, row_x, row_z, row_z, gx, gy)
    twiddle = table(row_x, col_x, row_z, col_z, gx * xl, gy * zl)
    inner = table(col_x, col_x, col_z, col_z, xl, zl)
    forward = np.block([[inner.real, inner.imag], [-inner.imag, inner.real]])
    return outer, twiddle, forward


def tables_back(gx, gh, gy, zl, xl):
    row_x, row_z = np.repeat(np.arange(gx), gh), np.tile(np.arange(gh), gx)
    layers = 2 * zl
    col_x, col_z = np.tile(np.arange(xl), layers), np.repeat(np.arange(layers), xl)
    edge = np.concatenate([np.arange(HALO), np.arange(xl - HALO, xl)])
    pick = (np.arange(layers)[:, None] * xl + edge).reshape(-1)
    freq_x = np.tile(np.arange(xl), layers)
    freq_z = np.repeat((np.arange(2)[:, None] + 2 * np.arange(zl)[None, :]).reshape(-1), xl)

    def table(left_x, right_x, left_z, right_z, size_x, size_z):
        phase = np.outer(left_x, right_x) / size_x + np.outer(left_z, right_z) / size_z
        return np.exp(2j * math.pi * phase)

    inner = table(freq_x, col_x, freq_z, col_z, xl, layers)
    twiddle = table(row_x, col_x, row_z, col_z, gx * xl, gh * layers)
    outer = table(row_x, row_x, row_z, row_z, gx, gh)
    blocks = [np.block([[t.real, t.imag], [-t.imag, t.real]]) for t in (inner, inner[:, pick])]
    edge_twiddle = twiddle[:, pick]
    edge_a = np.concatenate([edge_twiddle.real, edge_twiddle.real], axis=1)
    edge_b = np.concatenate([-edge_twiddle.imag, edge_twiddle.imag], axis=1)
    plain = [jnp.asarray(t, F32) for t in (twiddle.real, twiddle.imag, edge_a, edge_b)]
    return [*halves(np.concatenate(blocks, axis=1)), *plain, *halves(outer.real), *halves(outer.imag)]


def split(data):
    high = data.astype(BF16)
    return high, (data - high.astype(F32)).astype(BF16)


def dot(a, b):
    return jnp.dot(a, b, preferred_element_type=F32)


def left_product(table, data):
    (th, tl), (dh, dl) = table, data
    return dot(th, dh) + (dot(th, dl) + dot(tl, dh))


def right_product(data, table):
    (dh, dl), (th, tl) = data, table
    return dot(dh, th) + (dot(dl, th) + dot(dh, tl))


def mix_bits(seed_rows, cells):
    shift = lax.shift_right_logical
    hashed = seed_rows + cells * jnp.int32(-1640531535)
    hashed = hashed ^ shift(hashed, jnp.int32(16))
    hashed = hashed * jnp.int32(-2048144789)
    hashed = hashed ^ shift(hashed, jnp.int32(13))
    hashed = hashed * jnp.int32(-1028477387)
    hashed = hashed ^ shift(hashed, jnp.int32(16))
    value = shift(hashed, jnp.int32(8)).astype(F32)
    return (value + 0.5) * (2.0 * math.sqrt(3.0) / 16777216.0) - math.sqrt(3.0)


def noise_kernel(seed_ref, th_ref, tl_ref, out_ref):
    rows, half = th_ref.shape
    seeds = seed_ref[...]
    cells = lax.broadcasted_iota(jnp.int32, (half, seeds.shape[1]), 0)
    near = mix_bits(seeds, cells)
    far = mix_bits(seeds, cells + half)
    mid, count = rows // 2, half // 2
    for parity, data in enumerate((near + far, near - far)):
        at = slice(parity * mid, (parity + 1) * mid)
        product = left_product((th_ref[at], tl_ref[at]), split(data))
        out_ref[pl.ds(2 * parity, count, stride=4), :] = product[:count]
        out_ref[pl.ds(2 * parity + 1, count, stride=4), :] = product[count:]


def power(base, exponent):
    return jnp.exp(exponent * jnp.log(base))


def spectrum_kernel(sizes, device_ref, lengths_ref, exponents_ref, data_ref, ar_h, ar_l, ai_h, ai_l, tr_ref, ti_ref, fh_ref, fl_ref, bh_ref, bl_ref, br_ref, bi_ref, ea_ref, eb_ref, or_h, or_l, oi_h, oi_l, *rest):
    out_ref = rest[-1]
    gx, gy, zl, xl, length_y = sizes
    rows, cols = gx * gy, zl * xl
    outer_r = (ar_h[...], ar_l[...])
    outer_i = (ai_h[...], ai_l[...])
    tr, ti = tr_ref[...], ti_ref[...]
    shape = (rows, cols)
    row = lax.broadcasted_iota(jnp.int32, shape, 0)
    col = lax.broadcasted_iota(jnp.int32, shape, 1)
    kx = lax.div(row, gy) + gx * lax.rem(col, xl)
    kz = lax.rem(row, gy) + gy * lax.div(col, xl)
    ky = device_ref[0]

    def wave(index, length):
        folded = jnp.minimum(index, length - index)
        return folded.astype(F32) * (2.0 * math.pi / length)

    ky_all = jnp.full((8, cols), ky, jnp.int32)
    total_y = 1.0 + power(lengths_ref[2] * wave(ky_all, length_y), exponents_ref[2])
    weight = jnp.where(ky_all == 0, 1.0, 2.0)
    volume = jnp.full((8, cols), lengths_ref[0] * lengths_ref[1] * lengths_ref[2], F32)
    scale = 1.0 / (gx * xl * gy * zl * length_y)
    numerator = AMPLITUDE * jnp.sqrt(volume) * scale * weight
    total = power(lengths_ref[0] * wave(kz, gy * zl), exponents_ref[0])
    total = total + power(lengths_ref[1] * wave(kx, gx * xl), exponents_ref[1])
    gain = numerator[:1] / (total_y[:1] + total)
    data = jnp.concatenate([data_ref[pl.ds(0, rows, stride=2), :], data_ref[pl.ds(1, rows, stride=2), :]], axis=1)
    parts = split(data)
    pr, pi = left_product(outer_r, parts), left_product(outer_i, parts)
    yr, yi = pr[:, :cols] - pi[:, cols:], pr[:, cols:] + pi[:, :cols]
    data = jnp.concatenate([yr * tr - yi * ti, yr * ti + yi * tr], axis=1)
    data = right_product(split(data), (fh_ref[...], fl_ref[...]))
    data = data * jnp.concatenate([gain, gain], axis=1)
    chips = gy // 2
    count, wide = gx * chips, 2 * cols
    data = data.reshape(gx, gy, wide)
    low = data[:, :chips].reshape(count, wide)
    high = data[:, chips:].reshape(count, wide)
    data = jnp.concatenate([low[:, :cols], high[:, :cols], low[:, cols:], high[:, cols:]], axis=1)
    data = right_product(split(data), (bh_ref[...], bl_ref[...]))
    yr, yi, edge = data[:, :wide], data[:, wide : 2 * wide], data[:, 2 * wide :]
    tr, ti = br_ref[...], bi_ref[...]
    turn = edge.shape[1] // 2
    edge = edge * ea_ref[...] + pltpu.roll(edge, turn, 1) * eb_ref[...]
    parts = split(jnp.concatenate([yr * tr - yi * ti, yr * ti + yi * tr, edge], axis=1))
    pr = left_product((or_h[...], or_l[...]), parts)
    pi = left_product((oi_h[...], oi_l[...]), parts)
    lane = lax.broadcasted_iota(jnp.int32, edge.shape, 1)
    turned = pltpu.roll(pi[:, 2 * wide :], turn, 1)
    edge = pr[:, 2 * wide :] + jnp.where(lane < turn, -turned, turned)
    edge = jnp.where(lax.rem(lane, 2 * HALO) < HALO, pltpu.roll(edge, count - chips, 0), pltpu.roll(edge, chips, 0))
    out = jnp.concatenate([pr[:, :wide] - pi[:, wide : 2 * wide], pr[:, wide : 2 * wide] + pi[:, :wide], edge], axis=1)
    pieces = out.shape[1] // 128
    for piece in range(pieces):
        out_ref[pl.ds(piece, count, stride=pieces), :] = out[:, piece * 128 : (piece + 1) * 128]


def edge_rows(value, xl, low_ref, high_ref, base):
    for layer in range(value.shape[0] // xl):
        at = base + layer * HALO
        low_ref[at : at + HALO] = value[layer * xl : layer * xl + HALO]
        high_ref[at : at + HALO] = value[(layer + 1) * xl - HALO : (layer + 1) * xl]


def widen(value_ref, low_ref, high_ref, base, xl, out_ref):
    for layer in range(value_ref.shape[0] // xl):
        to, at = layer * (xl + 2 * HALO), base + layer * HALO
        out_ref[to : to + xl] = value_ref[layer * xl : (layer + 1) * xl]
        out_ref[to + xl : to + xl + HALO] = high_ref[at : at + HALO]
        out_ref[to + xl + HALO : to + xl + 2 * HALO] = low_ref[at : at + HALO]


def field_kernel(xl, core_ref, data_ref, th_ref, tl_ref, *refs):
    both_ref, own_ref, other_ref = refs[-3:]
    rows, half = th_ref.shape
    mid, count = rows // 2, half // 2
    pieces = data_ref.shape[0] // count
    data = jnp.concatenate([data_ref[pl.ds(piece, count, stride=pieces), :] for piece in range(pieces)], axis=1)
    turned = jnp.transpose(data)
    wide = (turned.shape[0] - 128) // 2
    edge = turned[2 * wide :]
    left = jnp.concatenate([turned[:wide], turned[wide : 2 * wide]], axis=1)
    edge = jnp.concatenate([edge[:64], edge[64:]], axis=1)
    core = core_ref[0]
    at = pl.ds(pl.multiple_of(core * mid, mid), mid)
    part = right_product(split(jnp.concatenate([left, edge], axis=0)), (th_ref[at, :], tl_ref[at, :]))
    layers = wide // xl // 2
    sums = []
    for side in range(2):
        found = []
        for layer in range(side * layers, (side + 1) * layers):
            found.append(part[layer * xl : (layer + 1) * xl])
            found.append(part[wide + layer * 2 * HALO : wide + (layer + 1) * 2 * HALO])
        sums.append(jnp.concatenate(found, axis=0))
    own = jnp.where(core == 0, sums[0], sums[1])
    other = jnp.where(core == 0, sums[1], sums[0])
    size = own.shape[0]
    own_ref[...] = own
    other_ref[...] = other
    both_ref[:size] = own
    both_ref[size:] = other


def rhs_kernel(xl, origin_ref, recharge_ref, cells_ref, rates_ref, storage_ref, rhs_ref, low_ref, high_ref):
    rows, length = recharge_ref.shape
    wells = cells_ref.shape[1]
    layer = cells_ref[0:1] - origin_ref[0]
    line = cells_ref[1:2] - origin_ref[1]
    inside = (line >= 0) & (line < xl)
    at = jnp.where(inside, layer * xl + line, -1)
    rate = jnp.where(lax.broadcasted_iota(jnp.int32, (rows, wells), 0) == at, rates_ref[...], 0.0)
    column = (lax.broadcasted_iota(jnp.int32, (length, wells), 0) == cells_ref[2:3]).astype(F32).astype(BF16)
    added = None
    for _ in range(3):
        part = rate.astype(BF16)
        rate = rate - part.astype(F32)
        product = lax.dot_general(part, column, (((1,), (1,)), ((), ())), preferred_element_type=F32)
        added = product if added is None else added + product
    rhs = recharge_ref[...] + added
    rhs_ref[...] = rhs
    edge_rows(storage_ref[...], xl, low_ref, high_ref, 0)
    edge_rows(rhs, xl, low_ref, high_ref, rows // xl * HALO)


def widen_pair_kernel(xl, storage_ref, rhs_ref, low_ref, high_ref, s_ref, r_ref, first_ref, last_ref):
    layers, wide = storage_ref.shape[0] // xl, xl + 2 * HALO
    widen(storage_ref, low_ref, high_ref, 0, xl, s_ref)
    widen(rhs_ref, low_ref, high_ref, layers * HALO, xl, r_ref)
    size = (layers - 1) * wide
    first_ref[:size] = s_ref[:size]
    first_ref[size:] = r_ref[:size]
    last_ref[:size] = s_ref[wide:]
    last_ref[size:] = r_ref[wide:]


def krylov_kernel(xl, edge_ref, core_ref, both_ref, swap_ref, far_a, far_b, s_ref, r_ref, sr_low, sr_high, log_ref, u0_out, u1_out, u2_out, u3_out, diag_out, mom_out, q_all, cz, cx, cy, inv, u0, u1, u2, u3, diag):
    wide, length = xl + 2 * HALO, s_ref.shape[1]
    own = s_ref.shape[0] // wide
    total = own + 2 * HALO
    z_lo, z_hi, x_lo, x_hi = (edge_ref[i] for i in range(4))
    row = lax.broadcasted_iota(jnp.int32, (wide, length), 0)
    lane = lax.broadcasted_iota(jnp.int32, (wide, length), 1)
    keep_x = jnp.where(row == xl - 1, x_hi, jnp.where(row == wide - 1, x_lo, 1.0))
    keep_y = jnp.where(lane == length - 1, 0.0, 1.0)

    def at(z):
        return pl.ds(z * wide, wide)

    core = core_ref[0]
    sign = jnp.where(core == 0, 1.0, -1.0)
    size, half = own * wide, length // 2
    first, second = slice(0, size), slice(size, 2 * size)
    full = slice(0, size)
    near = jnp.where(core == 0, 2 * size, 0)
    groups = (
        (both_ref, first, swap_ref, second, size),
        (both_ref, second, swap_ref, first, near),
        (far_a, full, far_b, full, 2 * size - near),
    )
    for group, (a_ref, a_at, b_ref, b_at, start) in enumerate(groups):
        to = pl.ds(pl.multiple_of(start, 8), size)
        a, b = a_ref[a_at], b_ref[b_at]
        lower, upper = a + b, (a - b) * sign
        q_all[to, :half] = 0.5 * jnp.exp(-lower)
        q_all[to, half:] = 0.5 * jnp.exp(-upper)
        if group == 0:
            for layer in range(own):
                log_ref[layer * xl : (layer + 1) * xl, :half] = lower[layer * wide : layer * wide + xl]
                log_ref[layer * xl : (layer + 1) * xl, half:] = upper[layer * wide : layer * wide + xl]

    def q_of(z):
        return q_all[at(z)]

    def pair_of(z):
        depth = own - 1
        if z < HALO:
            return sr_low[at(z - 1)], sr_low[at(depth + z - 1)]
        if z >= HALO + own:
            return sr_high[at(z - HALO - own)], sr_high[at(depth + z - HALO - own)]
        return s_ref[at(z - HALO)], r_ref[at(z - HALO)]

    def up_x(value):
        return pltpu.roll(value, wide - 1, 0)

    def down_x(value):
        return pltpu.roll(value, 1, 0)

    def up_y(value):
        return pltpu.roll(value, length - 1, 1)

    def down_y(value):
        return pltpu.roll(value, 1, 1)

    for z in range(total - 1):
        face = pl.reciprocal(q_of(z) + q_of(z + 1))
        if z == HALO - 1:
            face = face * z_lo
        if z == HALO + own - 1:
            face = face * z_hi
        cz[at(z)] = face
        if z == 0:
            continue
        q = q_of(z)
        storage, rhs = pair_of(z)
        face_x = pl.reciprocal(q + up_x(q)) * keep_x
        face_y = pl.reciprocal(q + up_y(q)) * keep_y
        cx[at(z)] = face_x
        cy[at(z)] = face_y
        d = storage + cz[at(z - 1)] + face + face_x + down_x(face_x) + face_y + down_y(face_y)
        inverse = pl.reciprocal(d)
        inv[at(z)] = inverse
        u0[at(z)] = rhs * inverse
        if HALO <= z < HALO + own:
            diag[pl.ds((z - HALO) * xl, xl)] = d[:xl]
    levels = (u0, u1, u2, u3)
    for level in range(3):
        old, new = levels[level], levels[level + 1]
        for z in range(2 + level, total - 2 - level):
            here, face_x, face_y = old[at(z)], cx[at(z)], cy[at(z)]
            flow = cz[at(z - 1)] * old[at(z - 1)] + cz[at(z)] * old[at(z + 1)]
            flow = flow + face_x * up_x(here) + down_x(face_x * here)
            flow = flow + face_y * up_y(here) + down_y(face_y * here)
            new[at(z)] = flow * inv[at(z)]
    sums = [None] * 6
    for z in range(HALO, HALO + own):
        to = pl.ds((z - HALO) * xl, xl)
        d = diag[to]
        values = [level[pl.ds(z * wide, xl)] for level in levels]
        for out, value in zip((u0_out, u1_out, u2_out, u3_out), values):
            out[to] = value
        diag_out[to] = d
        for i in range(6):
            if i % 2 == 0:
                weighted = d * values[i // 2]
            term = weighted * values[(i + 1) // 2]
            term = jnp.sum(term, axis=0, keepdims=True)
            sums[i] = term if sums[i] is None else sums[i] + term
    place = lax.broadcasted_iota(jnp.int32, (1, 128), 1)
    moments = jnp.zeros((1, 128), F32)
    for i in range(6):
        moments = jnp.where(place == i, jnp.sum(sums[i], axis=1, keepdims=True), moments)
    mom_out[...] = jnp.broadcast_to(moments, mom_out.shape)


def partial_kernel(in_ref, out_ref):
    out_ref[...] = jnp.broadcast_to(jnp.sum(in_ref[...], axis=0, keepdims=True), out_ref.shape)


def final_kernel(iters, mom_ref, u0, u1, u2, u3, diag_ref, pressure_ref, residual_ref):
    moments = jnp.sum(mom_ref[...], axis=0, keepdims=True)
    lane = lax.broadcasted_iota(jnp.int32, (1, 128), 1)
    nu = [jnp.sum(jnp.where(lane == i, moments, 0.0), axis=1, keepdims=True) for i in range(2 * iters)]

    def form(a, b):
        total = None
        for i, left in enumerate(a):
            for j, right in enumerate(b):
                term = left * right * nu[i + j]
                total = term if total is None else total + term
        return total

    one = jnp.ones((1, 1), F32)
    zero = jnp.zeros((1, 1), F32)
    precond, direction, pressure = [one], [one], [zero] * iters
    rz = nu[0]
    for it in range(iters):
        image = [
            (direction[i] if i < len(direction) else zero) - (direction[i - 1] if i > 0 else zero)
            for i in range(len(direction) + 1)
        ]
        alpha = rz / form(direction, image)
        pressure = [old + alpha * direction[i] if i < len(direction) else old for i, old in enumerate(pressure)]
        precond = [(precond[i] if i < len(precond) else zero) - alpha * image[i] for i in range(len(image))]
        if it + 1 < iters:
            new = form(precond, precond)
            beta = new / rz
            direction = [
                precond[i] + beta * direction[i] if i < len(direction) else precond[i] for i in range(len(precond))
            ]
            rz = new
    basis = [u0[...], u1[...], u2[...], u3[...]]
    pressure_ref[...] = pressure[0] * basis[0] + pressure[1] * basis[1] + pressure[2] * basis[2]
    total = precond[0] * basis[0] + precond[1] * basis[1] + precond[2] * basis[2] + precond[3] * basis[3]
    residual_ref[...] = diag_ref[...] * total


ITERS = 3


def exchange(low, high, axis):
    count = lax.axis_size(axis)
    up = [(i, i + 1) for i in range(count - 1)]
    down = [(i + 1, i) for i in range(count - 1)]
    return lax.ppermute(high, axis, up), lax.ppermute(low, axis, down)


def shards(seeds, lengths, exponents, storage, recharge, well_cells, well_rates):
    zl, xl, length_y = storage.shape
    gx, gh = lax.axis_size("gx"), lax.axis_size("gh")
    gy = 2 * gh
    assert zl == HALO and xl >= HALO
    rows, wide = zl * xl, xl + 2 * HALO
    block, middle, part = f32(rows, length_y), f32(zl * wide, length_y), f32(2 * (zl - 1) * wide, length_y)
    edge_pair = f32(2 * zl * HALO, length_y)
    at_x, at_y = lax.axis_index("gx"), lax.axis_index(("gh", "core"))
    device = (at_x * gy + at_y).reshape(1).astype(jnp.int32)
    origin = jnp.stack([at_y * zl, at_x * xl]).astype(jnp.int32)
    edges = jnp.stack([at_y > 0, at_y < gy - 1, at_x > 0, at_x < gx - 1]).astype(F32)
    core = lax.axis_index("core").reshape(1).astype(jnp.int32)
    smem = pl.BlockSpec(memory_space=pltpu.SMEM)
    vmem = pl.BlockSpec(memory_space=pltpu.VMEM)
    ty = halves(table_y(length_y))
    outer, twiddle, inner = tables_zx(gx, gy, zl, xl)
    tables = [*halves(outer.real), *halves(outer.imag), jnp.asarray(twiddle.real, F32), jnp.asarray(twiddle.imag, F32)]
    tables += [*halves(inner), *tables_back(gx, gh, gy, zl, xl)]

    def everywhere(array, axes):
        return on_chip(lax.all_to_all(array, axes, split_axis=0, concat_axis=0, tiled=True).reshape(-1, array.shape[-1] if array.ndim == 2 else 128))

    flat_storage = storage.reshape(rows, length_y)
    rhs, low, high = call(
        lambda *refs: rhs_kernel(xl, *refs),
        [block, edge_pair, edge_pair],
        origin,
        recharge.reshape(rows, length_y),
        well_cells,
        well_rates.reshape(1, -1),
        flat_storage,
        specs=[smem] + [vmem] * 4,
    )
    pair_x = exchange(low, high, "gx")
    wide_storage, wide_rhs, first, last = call(
        lambda *refs: widen_pair_kernel(xl, *refs), [middle, middle, part, part], flat_storage, rhs, *pair_x
    )
    pair_low, pair_high = exchange(first, last, ("gh", "core"))

    spectrum = call(noise_kernel, f32(length_y, rows), seeds.reshape(1, rows), *ty)
    spectrum = everywhere(spectrum, ("gx", "gh", "core"))
    chips, message = gx * gh, 4 * rows + 128
    spectrum = call(
        lambda *refs: spectrum_kernel((gx, gy, zl, xl, length_y), *refs),
        f32(chips * message // 128, 128),
        device,
        lengths,
        exponents,
        spectrum,
        *tables,
        *pair_x,
        specs=[smem, smem, smem] + [vmem] * (1 + len(tables)) + [pl.BlockSpec(memory_space=pl.ANY)] * 2,
    )
    spectrum = everywhere(spectrum.reshape(chips, 1, message), ("gx", "gh"))
    partial = f32(zl * wide, length_y // 2)
    both, own, other = call(
        lambda *refs: field_kernel(xl, *refs),
        [f32(2 * zl * wide, length_y // 2), partial, partial],
        core,
        spectrum,
        *ty,
        first,
        specs=[smem] + [vmem] * 3 + [pl.BlockSpec(memory_space=pl.ANY)],
    )
    far = [(2 * c, 2 * c + 2) for c in range(gh - 1)] + [(2 * c + 3, 2 * c + 1) for c in range(gh - 1)]
    beside = [(2 * c + 1, 2 * c + 2) for c in range(gh - 1)] + [(2 * c + 2, 2 * c + 1) for c in range(gh - 1)]
    far_a = on_chip(lax.ppermute(other, ("gh", "core"), far))
    far_b = on_chip(lax.ppermute(own, ("gh", "core"), beside))
    swap = on_chip(lax.ppermute(both, "core", [(0, 1), (1, 0)]))

    layers = zl + 2 * HALO
    log_perm, *basis, diag, moments = call(
        lambda *refs: krylov_kernel(xl, *refs),
        [block] * 6 + [f32(gx, 128)],
        edges,
        core,
        both,
        swap,
        far_a,
        far_b,
        wide_storage,
        wide_rhs,
        pair_low,
        pair_high,
        specs=[smem] * 2 + [vmem] * 8,
        scratch=[pltpu.VMEM((layers * wide, length_y), F32)] * 9 + [pltpu.VMEM((rows, length_y), F32)],
        limit=60,
    )
    moments = lax.all_to_all(moments, "gx", split_axis=0, concat_axis=0, tiled=True)
    moments = call(partial_kernel, f32(gy, 128), moments)
    moments = lax.all_to_all(moments, ("gh", "core"), split_axis=0, concat_axis=0, tiled=True)
    pressure, residual = call(
        lambda *refs: final_kernel(ITERS, *refs), [block, block], moments, *basis, diag
    )
    shape = storage.shape
    return (log_perm.reshape(shape), pressure.reshape(shape), residual.reshape(shape))


def solution(mesh):
    gx, gy = mesh.devices.shape
    mesh = jax.sharding.Mesh(mesh.devices.reshape(gx, gy // 2, 2), ("gx", "gh", "core"))
    z = ("gh", "core")
    block = P(z, "gx", None)
    placed = (P(z, "gx"), P(), P(), block, block, P(), P())
    return jax.shard_map(shards, mesh=mesh, in_specs=placed, out_specs=(block, block, block), check_vma=False)
```

```python
import math

import jax
import jax.numpy as jnp
import numpy as np
from jax import lax
from jax.experimental import pallas as pl
from jax.experimental.pallas import tpu as pltpu
from jax.sharding import PartitionSpec as P


AMPLITUDE = 4.0
BF16 = jnp.bfloat16
F32 = jnp.float32
INTERPRET = False
HALO = 4


def call(body, outs, *args, specs=None, scratch=(), limit=60):
    return pl.pallas_call(
        body,
        out_shape=outs,
        in_specs=specs or [pl.BlockSpec(memory_space=pltpu.VMEM)] * len(args),
        scratch_shapes=scratch,
        interpret=INTERPRET,
        compiler_params=pltpu.CompilerParams(vmem_limit_bytes=limit * 2**20),
    )(*args)


def f32(*shape):
    return jax.ShapeDtypeStruct(shape, F32)


def on_chip(array):
    return array if INTERPRET else pltpu.with_memory_space_constraint(array, pltpu.MemorySpace.VMEM)


def halves(table):
    high = table.astype(BF16)
    low = (table - high.astype(np.float64)).astype(BF16)
    return jnp.asarray(high), jnp.asarray(low)


def cosine_sine(product, length):
    angle = (product % length).astype(np.float64) * (2.0 * math.pi / length)
    return np.cos(angle), np.sin(angle)


def table_y(length):
    half = length // 2
    k = np.arange(half).reshape(half // 2, 2).T
    cos, sin = cosine_sine(k[:, :, None] * np.arange(half), length)
    return np.stack([cos, -sin], axis=1).reshape(2 * half, half)


def tables_zx(gx, gy, zl, xl):
    row_x, row_z = np.repeat(np.arange(gx), gy), np.tile(np.arange(gy), gx)
    col_x, col_z = np.tile(np.arange(xl), zl), np.repeat(np.arange(zl), xl)

    def table(left_x, right_x, left_z, right_z, size_x, size_z):
        phase = np.outer(left_x, right_x) / size_x + np.outer(left_z, right_z) / size_z
        return np.exp(-2j * math.pi * phase)

    outer = table(row_x, row_x, row_z, row_z, gx, gy)
    twiddle = table(row_x, col_x, row_z, col_z, gx * xl, gy * zl)
    inner = table(col_x, col_x, col_z, col_z, xl, zl)
    forward = np.block([[inner.real, inner.imag], [-inner.imag, inner.real]])
    return outer, twiddle, forward


def tables_back(gx, gh, zl, xl):
    row_x, row_z = np.repeat(np.arange(gx), gh), np.tile(np.arange(gh), gx)
    layers = 2 * zl
    col_x, col_z = np.tile(np.arange(xl), layers), np.repeat(np.arange(layers), xl)
    edge = np.concatenate([np.arange(HALO), np.arange(xl - HALO, xl)])
    pick = (np.arange(layers)[:, None] * xl + edge).reshape(-1)
    freq_x = np.tile(np.arange(xl), layers)
    freq_z = np.repeat((np.arange(2)[:, None] + 2 * np.arange(zl)[None, :]).reshape(-1), xl)

    def table(left_x, right_x, left_z, right_z, size_x, size_z):
        phase = np.outer(left_x, right_x) / size_x + np.outer(left_z, right_z) / size_z
        return np.exp(2j * math.pi * phase)

    inner = table(freq_x, col_x, freq_z, col_z, xl, layers)
    twiddle = table(row_x, col_x, row_z, col_z, gx * xl, gh * layers)
    outer = table(row_x, row_x, row_z, row_z, gx, gh)
    blocks = [np.block([[t.real, t.imag], [-t.imag, t.real]]) for t in (inner, inner[:, pick])]
    edge_twiddle = twiddle[:, pick]
    edge_a = np.concatenate([edge_twiddle.real, edge_twiddle.real], axis=1)
    edge_b = np.concatenate([-edge_twiddle.imag, edge_twiddle.imag], axis=1)
    plain = [jnp.asarray(t, F32) for t in (twiddle.real, twiddle.imag, edge_a, edge_b)]
    return [*halves(np.concatenate(blocks, axis=1)), *plain, *halves(outer.real), *halves(outer.imag)]


def split(data):
    high = data.astype(BF16)
    return high, (data - high.astype(F32)).astype(BF16)


def dot(a, b):
    return jnp.dot(a, b, preferred_element_type=F32)


def left_product(table, data):
    (th, tl), (dh, dl) = table, data
    return dot(th, dh) + (dot(th, dl) + dot(tl, dh))


def right_product(data, table):
    (dh, dl), (th, tl) = data, table
    return dot(dh, th) + (dot(dl, th) + dot(dh, tl))


def mix_bits(seed_rows, cells):
    shift = lax.shift_right_logical
    hashed = seed_rows + cells * jnp.int32(-1640531535)
    hashed = hashed ^ shift(hashed, jnp.int32(16))
    hashed = hashed * jnp.int32(-2048144789)
    hashed = hashed ^ shift(hashed, jnp.int32(13))
    hashed = hashed * jnp.int32(-1028477387)
    hashed = hashed ^ shift(hashed, jnp.int32(16))
    value = shift(hashed, jnp.int32(8)).astype(F32)
    return (value + 0.5) * (2.0 * math.sqrt(3.0) / 16777216.0) - math.sqrt(3.0)


def noise_kernel(seed_ref, th_ref, tl_ref, out_ref):
    rows, half = th_ref.shape
    seeds = jnp.concatenate([seed_ref[layer : layer + 1] for layer in range(seed_ref.shape[0])], axis=1)
    cells = lax.broadcasted_iota(jnp.int32, (half, seeds.shape[1]), 0)
    near = mix_bits(seeds, cells)
    far = mix_bits(seeds, cells + half)
    mid, count = rows // 2, half // 2
    for parity, data in enumerate((near + far, near - far)):
        at = slice(parity * mid, (parity + 1) * mid)
        product = left_product((th_ref[at], tl_ref[at]), split(data))
        out_ref[pl.ds(2 * parity, count, stride=4), :] = product[:count]
        out_ref[pl.ds(2 * parity + 1, count, stride=4), :] = product[count:]


def power(base, exponent):
    return jnp.exp(exponent * jnp.log(base))


def spectrum_kernel(sizes, device_ref, lengths_ref, exponents_ref, data_ref, ar_h, ar_l, ai_h, ai_l, tr_ref, ti_ref, fh_ref, fl_ref, bh_ref, bl_ref, br_ref, bi_ref, ea_ref, eb_ref, or_h, or_l, oi_h, oi_l, *rest):
    out_ref = rest[-1]
    gx, gy, zl, xl, length_y = sizes
    rows, cols = gx * gy, zl * xl
    outer_r = (ar_h[...], ar_l[...])
    outer_i = (ai_h[...], ai_l[...])
    tr, ti = tr_ref[...], ti_ref[...]
    shape = (rows, cols)
    row = lax.broadcasted_iota(jnp.int32, shape, 0)
    col = lax.broadcasted_iota(jnp.int32, shape, 1)
    kx = lax.div(row, gy) + gx * lax.rem(col, xl)
    kz = lax.rem(row, gy) + gy * lax.div(col, xl)
    ky = device_ref[0]

    def wave(index, length):
        folded = jnp.minimum(index, length - index)
        return folded.astype(F32) * (2.0 * math.pi / length)

    ky_all = jnp.full((8, cols), ky, jnp.int32)
    total_y = 1.0 + power(lengths_ref[2] * wave(ky_all, length_y), exponents_ref[2])
    weight = jnp.where(ky_all == 0, 1.0, 2.0)
    volume = jnp.full((8, cols), lengths_ref[0] * lengths_ref[1] * lengths_ref[2], F32)
    scale = 1.0 / (gx * xl * gy * zl * length_y)
    numerator = AMPLITUDE * jnp.sqrt(volume) * scale * weight
    total = power(lengths_ref[0] * wave(kz, gy * zl), exponents_ref[0])
    total = total + power(lengths_ref[1] * wave(kx, gx * xl), exponents_ref[1])
    gain = numerator[:1] / (total_y[:1] + total)
    data = jnp.concatenate([data_ref[pl.ds(0, rows, stride=2), :], data_ref[pl.ds(1, rows, stride=2), :]], axis=1)
    parts = split(data)
    pr, pi = left_product(outer_r, parts), left_product(outer_i, parts)
    yr, yi = pr[:, :cols] - pi[:, cols:], pr[:, cols:] + pi[:, :cols]
    data = jnp.concatenate([yr * tr - yi * ti, yr * ti + yi * tr], axis=1)
    data = right_product(split(data), (fh_ref[...], fl_ref[...]))
    data = data * jnp.concatenate([gain, gain], axis=1)
    chips = gy // 2
    count, wide = gx * chips, 2 * cols
    data = data.reshape(gx, gy, wide)
    low = data[:, :chips].reshape(count, wide)
    high = data[:, chips:].reshape(count, wide)
    data = jnp.concatenate([low[:, :cols], high[:, :cols], low[:, cols:], high[:, cols:]], axis=1)
    data = right_product(split(data), (bh_ref[...], bl_ref[...]))
    yr, yi, edge = data[:, :wide], data[:, wide : 2 * wide], data[:, 2 * wide :]
    tr, ti = br_ref[...], bi_ref[...]
    turn = edge.shape[1] // 2
    edge = edge * ea_ref[...] + pltpu.roll(edge, turn, 1) * eb_ref[...]
    parts = split(jnp.concatenate([yr * tr - yi * ti, yr * ti + yi * tr, edge], axis=1))
    pr = left_product((or_h[...], or_l[...]), parts)
    pi = left_product((oi_h[...], oi_l[...]), parts)
    lane = lax.broadcasted_iota(jnp.int32, edge.shape, 1)
    turned = pltpu.roll(pi[:, 2 * wide :], turn, 1)
    edge = pr[:, 2 * wide :] + jnp.where(lane < turn, -turned, turned)
    edge = jnp.where(lax.rem(lane, 2 * HALO) < HALO, pltpu.roll(edge, count - chips, 0), pltpu.roll(edge, chips, 0))
    out = jnp.concatenate([pr[:, :wide] - pi[:, wide : 2 * wide], pr[:, wide : 2 * wide] + pi[:, :wide], edge], axis=1)
    pieces = out.shape[1] // 128
    for piece in range(pieces):
        out_ref[pl.ds(piece, count, stride=pieces), :] = out[:, piece * 128 : (piece + 1) * 128]


def edge_rows(value, xl, low_ref, high_ref, base):
    for layer in range(value.shape[0] // xl):
        at = base + layer * HALO
        low_ref[at : at + HALO] = value[layer * xl : layer * xl + HALO]
        high_ref[at : at + HALO] = value[(layer + 1) * xl - HALO : (layer + 1) * xl]


def widen(value_ref, low_ref, high_ref, base, xl, out_ref):
    for layer in range(value_ref.shape[0] // xl):
        to, at = layer * (xl + 2 * HALO), base + layer * HALO
        out_ref[to : to + xl] = value_ref[layer * xl : (layer + 1) * xl]
        out_ref[to + xl : to + xl + HALO] = high_ref[at : at + HALO]
        out_ref[to + xl + HALO : to + xl + 2 * HALO] = low_ref[at : at + HALO]


def field_kernel(xl, device_ref, data_ref, th_ref, tl_ref, *refs):
    both_ref, own_ref, other_ref = refs[-3:]
    rows, half = th_ref.shape
    mid, count = rows // 2, half // 2
    pieces = data_ref.shape[0] // count
    data = jnp.concatenate([data_ref[pl.ds(piece, count, stride=pieces), :] for piece in range(pieces)], axis=1)
    turned = jnp.transpose(data)
    wide = (turned.shape[0] - 128) // 2
    edge = turned[2 * wide :]
    left = jnp.concatenate([turned[:wide], turned[wide : 2 * wide]], axis=1)
    edge = jnp.concatenate([edge[:64], edge[64:]], axis=1)
    core = lax.rem(device_ref[0], 2)
    at = pl.ds(pl.multiple_of(core * mid, mid), mid)
    part = right_product(split(jnp.concatenate([left, edge], axis=0)), (th_ref[at, :], tl_ref[at, :]))
    layers = wide // xl // 2
    sums = []
    for side in range(2):
        found = []
        for layer in range(side * layers, (side + 1) * layers):
            found.append(part[layer * xl : (layer + 1) * xl])
            found.append(part[wide + layer * 2 * HALO : wide + (layer + 1) * 2 * HALO])
        sums.append(jnp.concatenate(found, axis=0))
    own = jnp.where(core == 0, sums[0], sums[1])
    other = jnp.where(core == 0, sums[1], sums[0])
    size = own.shape[0]
    own_ref[...] = own
    other_ref[...] = other
    both_ref[:size] = own
    both_ref[size:] = other


def rhs_kernel(xl, gy, device_ref, recharge_ref, cells_ref, rates_ref, storage_ref, rhs_ref, low_ref, high_ref):
    rows, length = recharge_ref.shape
    wells = cells_ref.shape[1]
    at_x, at_y = lax.div(device_ref[0], gy), lax.rem(device_ref[0], gy)
    layer = cells_ref[0:1] - at_y * (rows // xl)
    line = cells_ref[1:2] - at_x * xl
    inside = (line >= 0) & (line < xl)
    at = jnp.where(inside, layer * xl + line, -1)
    rate = jnp.where(lax.broadcasted_iota(jnp.int32, (rows, wells), 0) == at, rates_ref[...], 0.0)
    column = (lax.broadcasted_iota(jnp.int32, (length, wells), 0) == cells_ref[2:3]).astype(F32).astype(BF16)
    added = None
    for _ in range(3):
        part = rate.astype(BF16)
        rate = rate - part.astype(F32)
        product = lax.dot_general(part, column, (((1,), (1,)), ((), ())), preferred_element_type=F32)
        added = product if added is None else added + product
    rhs = recharge_ref[...] + added
    rhs_ref[...] = rhs
    edge_rows(storage_ref[...], xl, low_ref, high_ref, 0)
    edge_rows(rhs, xl, low_ref, high_ref, rows // xl * HALO)


def widen_pair_kernel(xl, storage_ref, rhs_ref, low_ref, high_ref, s_ref, r_ref, first_ref, last_ref):
    layers, wide = storage_ref.shape[0] // xl, xl + 2 * HALO
    widen(storage_ref, low_ref, high_ref, 0, xl, s_ref)
    widen(rhs_ref, low_ref, high_ref, layers * HALO, xl, r_ref)
    size = (layers - 1) * wide
    first_ref[:size] = s_ref[:size]
    first_ref[size:] = r_ref[:size]
    last_ref[:size] = s_ref[wide:]
    last_ref[size:] = r_ref[wide:]


def krylov_kernel(xl, gx, gy, device_ref, both_ref, swap_ref, far_a, far_b, s_ref, r_ref, sr_low, sr_high, log_ref, u0_out, u1_out, u2_out, u3_out, diag_out, mom_out, q_all, cz, cx, cy, inv, u0, u1, u2, u3, diag):
    wide, length = xl + 2 * HALO, s_ref.shape[1]
    own = s_ref.shape[0] // wide
    total = own + 2 * HALO
    at_x, at_y = lax.div(device_ref[0], gy), lax.rem(device_ref[0], gy)
    sides = (at_y > 0, at_y < gy - 1, at_x > 0, at_x < gx - 1)
    z_lo, z_hi, x_lo, x_hi = (jnp.where(side, 1.0, 0.0) for side in sides)
    row = lax.broadcasted_iota(jnp.int32, (wide, length), 0)
    lane = lax.broadcasted_iota(jnp.int32, (wide, length), 1)
    keep_x = jnp.where(row == xl - 1, x_hi, jnp.where(row == wide - 1, x_lo, 1.0))
    keep_y = jnp.where(lane == length - 1, 0.0, 1.0)

    def at(z):
        return pl.ds(z * wide, wide)

    core = lax.rem(device_ref[0], 2)
    sign = jnp.where(core == 0, 1.0, -1.0)
    size, half = own * wide, length // 2
    first, second = slice(0, size), slice(size, 2 * size)
    full = slice(0, size)
    near = jnp.where(core == 0, 2 * size, 0)
    groups = (
        (both_ref, first, swap_ref, second, size),
        (both_ref, second, swap_ref, first, near),
        (far_a, full, far_b, full, 2 * size - near),
    )
    for group, (a_ref, a_at, b_ref, b_at, start) in enumerate(groups):
        to = pl.ds(pl.multiple_of(start, 8), size)
        a, b = a_ref[a_at], b_ref[b_at]
        lower, upper = a + b, (a - b) * sign
        q_all[to, :half] = 0.5 * jnp.exp(-lower)
        q_all[to, half:] = 0.5 * jnp.exp(-upper)
        if group == 0:
            for layer in range(own):
                log_ref[layer * xl : (layer + 1) * xl, :half] = lower[layer * wide : layer * wide + xl]
                log_ref[layer * xl : (layer + 1) * xl, half:] = upper[layer * wide : layer * wide + xl]

    def q_of(z):
        return q_all[at(z)]

    def pair_of(z):
        depth = own - 1
        if z < HALO:
            return sr_low[at(z - 1)], sr_low[at(depth + z - 1)]
        if z >= HALO + own:
            return sr_high[at(z - HALO - own)], sr_high[at(depth + z - HALO - own)]
        return s_ref[at(z - HALO)], r_ref[at(z - HALO)]

    def up_x(value):
        return pltpu.roll(value, wide - 1, 0)

    def down_x(value):
        return pltpu.roll(value, 1, 0)

    def up_y(value):
        return pltpu.roll(value, length - 1, 1)

    def down_y(value):
        return pltpu.roll(value, 1, 1)

    for z in range(total - 1):
        face = pl.reciprocal(q_of(z) + q_of(z + 1))
        if z == HALO - 1:
            face = face * z_lo
        if z == HALO + own - 1:
            face = face * z_hi
        cz[at(z)] = face
        if z == 0:
            continue
        q = q_of(z)
        storage, rhs = pair_of(z)
        face_x = pl.reciprocal(q + up_x(q)) * keep_x
        face_y = pl.reciprocal(q + up_y(q)) * keep_y
        cx[at(z)] = face_x
        cy[at(z)] = face_y
        d = storage + cz[at(z - 1)] + face + face_x + down_x(face_x) + face_y + down_y(face_y)
        inverse = pl.reciprocal(d)
        inv[at(z)] = inverse
        u0[at(z)] = rhs * inverse
        if HALO <= z < HALO + own:
            diag[pl.ds((z - HALO) * xl, xl)] = d[:xl]
    levels = (u0, u1, u2, u3)
    for level in range(3):
        old, new = levels[level], levels[level + 1]
        for z in range(2 + level, total - 2 - level):
            here, face_x, face_y = old[at(z)], cx[at(z)], cy[at(z)]
            flow = cz[at(z - 1)] * old[at(z - 1)] + cz[at(z)] * old[at(z + 1)]
            flow = flow + face_x * up_x(here) + down_x(face_x * here)
            flow = flow + face_y * up_y(here) + down_y(face_y * here)
            new[at(z)] = flow * inv[at(z)]
    sums = [None] * 6
    for z in range(HALO, HALO + own):
        to = pl.ds((z - HALO) * xl, xl)
        d = diag[to]
        values = [level[pl.ds(z * wide, xl)] for level in levels]
        for out, value in zip((u0_out, u1_out, u2_out, u3_out), values):
            out[to] = value
        diag_out[to] = d
        for i in range(6):
            if i % 2 == 0:
                weighted = d * values[i // 2]
            term = weighted * values[(i + 1) // 2]
            term = jnp.sum(term, axis=0, keepdims=True)
            sums[i] = term if sums[i] is None else sums[i] + term
    place = lax.broadcasted_iota(jnp.int32, (1, 128), 1)
    moments = jnp.zeros((1, 128), F32)
    for i in range(6):
        moments = jnp.where(place == i, jnp.sum(sums[i], axis=1, keepdims=True), moments)
    mom_out[...] = jnp.broadcast_to(moments, mom_out.shape)


def partial_kernel(in_ref, out_ref):
    out_ref[...] = jnp.broadcast_to(jnp.sum(in_ref[...], axis=0, keepdims=True), out_ref.shape)


def final_kernel(iters, mom_ref, u0, u1, u2, u3, diag_ref, pressure_ref, residual_ref):
    moments = jnp.sum(mom_ref[...], axis=0, keepdims=True)
    lane = lax.broadcasted_iota(jnp.int32, (1, 128), 1)
    nu = [jnp.sum(jnp.where(lane == i, moments, 0.0), axis=1, keepdims=True) for i in range(2 * iters)]

    def form(a, b):
        total = None
        for i, left in enumerate(a):
            for j, right in enumerate(b):
                term = left * right * nu[i + j]
                total = term if total is None else total + term
        return total

    one = jnp.ones((1, 1), F32)
    zero = jnp.zeros((1, 1), F32)
    precond, direction, pressure = [one], [one], [zero] * iters
    rz = nu[0]
    for it in range(iters):
        image = [
            (direction[i] if i < len(direction) else zero) - (direction[i - 1] if i > 0 else zero)
            for i in range(len(direction) + 1)
        ]
        alpha = rz / form(direction, image)
        pressure = [old + alpha * direction[i] if i < len(direction) else old for i, old in enumerate(pressure)]
        precond = [(precond[i] if i < len(precond) else zero) - alpha * image[i] for i in range(len(image))]
        if it + 1 < iters:
            new = form(precond, precond)
            beta = new / rz
            direction = [
                precond[i] + beta * direction[i] if i < len(direction) else precond[i] for i in range(len(precond))
            ]
            rz = new
    basis = [u0[...], u1[...], u2[...], u3[...]]
    pressure_ref[...] = pressure[0] * basis[0] + pressure[1] * basis[1] + pressure[2] * basis[2]
    total = precond[0] * basis[0] + precond[1] * basis[1] + precond[2] * basis[2] + precond[3] * basis[3]
    residual_ref[...] = diag_ref[...] * total


ITERS = 3


def exchange(low, high, axis):
    count = lax.axis_size(axis)
    up = [(i, i + 1) for i in range(count - 1)]
    down = [(i + 1, i) for i in range(count - 1)]
    from_low = lax.ppermute(high, axis, up)
    return from_low, lax.ppermute(low, axis, down)


def shards(seeds, lengths, exponents, storage, recharge, well_cells, well_rates):
    zl, xl, length_y = storage.shape
    gx, gh = lax.axis_size("gx"), lax.axis_size("gh")
    gy = 2 * gh
    assert zl == HALO and xl >= HALO
    rows, wide = zl * xl, xl + 2 * HALO
    block, middle, part = f32(rows, length_y), f32(zl * wide, length_y), f32(2 * (zl - 1) * wide, length_y)
    edge_pair = f32(2 * zl * HALO, length_y)
    at_x, at_y = lax.axis_index("gx"), lax.axis_index(("gh", "core"))
    device = (at_x * gy + at_y).reshape(1).astype(jnp.int32)
    smem = pl.BlockSpec(memory_space=pltpu.SMEM)
    vmem = pl.BlockSpec(memory_space=pltpu.VMEM)
    ty = halves(table_y(length_y))
    outer, twiddle, inner = tables_zx(gx, gy, zl, xl)
    tables = [*halves(outer.real), *halves(outer.imag), jnp.asarray(twiddle.real, F32), jnp.asarray(twiddle.imag, F32)]
    tables += [*halves(inner), *tables_back(gx, gh, zl, xl)]

    def everywhere(array, axes):
        return on_chip(lax.all_to_all(array, axes, split_axis=0, concat_axis=0, tiled=True).reshape(-1, array.shape[-1] if array.ndim == 2 else 128))

    flat_storage = storage.reshape(rows, length_y)
    rhs, low, high = call(
        lambda *refs: rhs_kernel(xl, gy, *refs),
        [block, edge_pair, edge_pair],
        device,
        recharge.reshape(rows, length_y),
        well_cells,
        well_rates.reshape(1, -1),
        flat_storage,
        specs=[smem] + [vmem] * 4,
    )
    pair_x = exchange(low, high, "gx")
    wide_storage, wide_rhs, first, last = call(
        lambda *refs: widen_pair_kernel(xl, *refs), [middle, middle, part, part], flat_storage, rhs, *pair_x
    )
    pair_low, pair_high = exchange(first, last, ("gh", "core"))

    spectrum = call(noise_kernel, f32(length_y, rows), seeds, *ty)
    spectrum = everywhere(spectrum, ("gx", "gh", "core"))
    chips, message = gx * gh, 4 * rows + 128
    spectrum = call(
        lambda *refs: spectrum_kernel((gx, gy, zl, xl, length_y), *refs),
        f32(chips * message // 128, 128),
        device,
        lengths,
        exponents,
        spectrum,
        *tables,
        specs=[smem, smem, smem] + [vmem] * (1 + len(tables)),
    )
    spectrum = everywhere(spectrum.reshape(chips, 1, message), ("gx", "gh"))
    partial = f32(zl * wide, length_y // 2)
    both, own, other = call(
        lambda *refs: field_kernel(xl, *refs),
        [f32(2 * zl * wide, length_y // 2), partial, partial],
        device,
        spectrum,
        *ty,
        first,
        specs=[smem] + [vmem] * 3 + [pl.BlockSpec(memory_space=pl.ANY)],
    )
    far = [(2 * c, 2 * c + 2) for c in range(gh - 1)] + [(2 * c + 3, 2 * c + 1) for c in range(gh - 1)]
    beside = [(2 * c + 1, 2 * c + 2) for c in range(gh - 1)] + [(2 * c + 2, 2 * c + 1) for c in range(gh - 1)]
    far_a = on_chip(lax.ppermute(other, ("gh", "core"), far))
    far_b = on_chip(lax.ppermute(own, ("gh", "core"), beside))
    swap = on_chip(lax.ppermute(both, "core", [(0, 1), (1, 0)]))

    layers = zl + 2 * HALO
    log_perm, *basis, diag, moments = call(
        lambda *refs: krylov_kernel(xl, gx, gy, *refs),
        [block] * 6 + [f32(gx, 128)],
        device,
        both,
        swap,
        far_a,
        far_b,
        wide_storage,
        wide_rhs,
        pair_low,
        pair_high,
        specs=[smem] + [vmem] * 8,
        scratch=[pltpu.VMEM((layers * wide, length_y), F32)] * 9 + [pltpu.VMEM((rows, length_y), F32)],
        limit=60,
    )
    moments = lax.all_to_all(moments, "gx", split_axis=0, concat_axis=0, tiled=True)
    moments = call(partial_kernel, f32(gy, 128), moments)
    moments = lax.all_to_all(moments, ("gh", "core"), split_axis=0, concat_axis=0, tiled=True)
    pressure, residual = call(
        lambda *refs: final_kernel(ITERS, *refs), [block, block], moments, *basis, diag
    )
    shape = storage.shape
    return (log_perm.reshape(shape), pressure.reshape(shape), residual.reshape(shape))


def solution(mesh):
    gx, gy = mesh.devices.shape
    mesh = jax.sharding.Mesh(mesh.devices.reshape(gx, gy // 2, 2), ("gx", "gh", "core"))
    z = ("gh", "core")
    block = P(z, "gx", None)
    placed = (P(z, "gx"), P(), P(), block, block, P(), P())

    return jax.shard_map(shards, mesh=mesh, in_specs=placed, out_specs=(block, block, block), check_vma=False)
```

```python
import math

import jax
import jax.numpy as jnp
import numpy as np
from jax import lax
from jax.experimental import pallas as pl
from jax.experimental.pallas import tpu as pltpu
from jax.sharding import PartitionSpec as P


AMPLITUDE = 4.0
BF16 = jnp.bfloat16
F32 = jnp.float32
INTERPRET = False
HALO = 4


def call(body, outs, *args, specs=None, scratch=(), limit=60):
    return pl.pallas_call(
        body,
        out_shape=outs,
        in_specs=specs or [pl.BlockSpec(memory_space=pltpu.VMEM)] * len(args),
        scratch_shapes=scratch,
        interpret=INTERPRET,
        compiler_params=pltpu.CompilerParams(vmem_limit_bytes=limit * 2**20),
    )(*args)


def f32(*shape):
    return jax.ShapeDtypeStruct(shape, F32)


def on_chip(array):
    return array if INTERPRET else pltpu.with_memory_space_constraint(array, pltpu.MemorySpace.VMEM)


def halves(table):
    high = table.astype(BF16)
    low = (table - high.astype(np.float64)).astype(BF16)
    return jnp.asarray(high), jnp.asarray(low)


def cosine_sine(product, length):
    angle = (product % length).astype(np.float64) * (2.0 * math.pi / length)
    return np.cos(angle), np.sin(angle)


def table_y(length):
    half = length // 2
    k = np.arange(half).reshape(half // 2, 2).T
    cos, sin = cosine_sine(k[:, :, None] * np.arange(half), length)
    return np.stack([cos, -sin], axis=1).reshape(2 * half, half)


def tables_zx(gx, gy, zl, xl):
    row_x, row_z = np.repeat(np.arange(gx), gy), np.tile(np.arange(gy), gx)
    col_x, col_z = np.tile(np.arange(xl), zl), np.repeat(np.arange(zl), xl)

    def table(left_x, right_x, left_z, right_z, size_x, size_z):
        phase = np.outer(left_x, right_x) / size_x + np.outer(left_z, right_z) / size_z
        return np.exp(-2j * math.pi * phase)

    outer = table(row_x, row_x, row_z, row_z, gx, gy)
    twiddle = table(row_x, col_x, row_z, col_z, gx * xl, gy * zl)
    inner = table(col_x, col_x, col_z, col_z, xl, zl)
    forward = np.block([[inner.real, inner.imag], [-inner.imag, inner.real]])
    return outer, twiddle, forward


def tables_back(gx, gh, zl, xl):
    row_x, row_z = np.repeat(np.arange(gx), gh), np.tile(np.arange(gh), gx)
    layers = 2 * zl
    col_x, col_z = np.tile(np.arange(xl), layers), np.repeat(np.arange(layers), xl)
    edge = np.concatenate([np.arange(HALO), np.arange(xl - HALO, xl)])
    pick = (np.arange(layers)[:, None] * xl + edge).reshape(-1)
    freq_x = np.tile(np.arange(xl), layers)
    freq_z = np.repeat((np.arange(2)[:, None] + 2 * np.arange(zl)[None, :]).reshape(-1), xl)

    def table(left_x, right_x, left_z, right_z, size_x, size_z):
        phase = np.outer(left_x, right_x) / size_x + np.outer(left_z, right_z) / size_z
        return np.exp(2j * math.pi * phase)

    inner = table(freq_x, col_x, freq_z, col_z, xl, layers)
    twiddle = table(row_x, col_x, row_z, col_z, gx * xl, gh * layers)
    outer = table(row_x, row_x, row_z, row_z, gx, gh)
    blocks = [np.block([[t.real, t.imag], [-t.imag, t.real]]) for t in (inner, inner[:, pick])]
    edge_twiddle = twiddle[:, pick]
    edge_a = np.concatenate([edge_twiddle.real, edge_twiddle.real], axis=1)
    edge_b = np.concatenate([-edge_twiddle.imag, edge_twiddle.imag], axis=1)
    plain = [jnp.asarray(t, F32) for t in (twiddle.real, twiddle.imag, edge_a, edge_b)]
    return [*halves(np.concatenate(blocks, axis=1)), *plain, *halves(outer.real), *halves(outer.imag)]


def split(data):
    high = data.astype(BF16)
    return high, (data - high.astype(F32)).astype(BF16)


def dot(a, b):
    return jnp.dot(a, b, preferred_element_type=F32)


def left_product(table, data):
    (th, tl), (dh, dl) = table, data
    return dot(th, dh) + (dot(th, dl) + dot(tl, dh))


def right_product(data, table):
    (dh, dl), (th, tl) = data, table
    return dot(dh, th) + (dot(dl, th) + dot(dh, tl))


def mix_bits(seed_rows, cells):
    shift = lax.shift_right_logical
    hashed = seed_rows + cells * jnp.int32(-1640531535)
    hashed = hashed ^ shift(hashed, jnp.int32(16))
    hashed = hashed * jnp.int32(-2048144789)
    hashed = hashed ^ shift(hashed, jnp.int32(13))
    hashed = hashed * jnp.int32(-1028477387)
    hashed = hashed ^ shift(hashed, jnp.int32(16))
    value = shift(hashed, jnp.int32(8)).astype(F32)
    return (value + 0.5) * (2.0 * math.sqrt(3.0) / 16777216.0) - math.sqrt(3.0)


def noise_kernel(seed_ref, th_ref, tl_ref, out_ref):
    rows, half = th_ref.shape
    seeds = jnp.concatenate([seed_ref[layer : layer + 1] for layer in range(seed_ref.shape[0])], axis=1)
    cells = lax.broadcasted_iota(jnp.int32, (half, seeds.shape[1]), 0)
    near = mix_bits(seeds, cells)
    far = mix_bits(seeds, cells + half)
    mid, count = rows // 2, half // 2
    for parity, data in enumerate((near + far, near - far)):
        at = slice(parity * mid, (parity + 1) * mid)
        product = left_product((th_ref[at], tl_ref[at]), split(data))
        out_ref[pl.ds(2 * parity, count, stride=4), :] = product[:count]
        out_ref[pl.ds(2 * parity + 1, count, stride=4), :] = product[count:]


def power(base, exponent):
    return jnp.exp(exponent * jnp.log(base))


def spectrum_kernel(sizes, device_ref, lengths_ref, exponents_ref, data_ref, ar_h, ar_l, ai_h, ai_l, tr_ref, ti_ref, fh_ref, fl_ref, bh_ref, bl_ref, br_ref, bi_ref, ea_ref, eb_ref, or_h, or_l, oi_h, oi_l, *rest):
    out_ref = rest[-1]
    gx, gy, zl, xl, length_y = sizes
    rows, cols = gx * gy, zl * xl
    outer_r = (ar_h[...], ar_l[...])
    outer_i = (ai_h[...], ai_l[...])
    tr, ti = tr_ref[...], ti_ref[...]
    shape = (rows, cols)
    row = lax.broadcasted_iota(jnp.int32, shape, 0)
    col = lax.broadcasted_iota(jnp.int32, shape, 1)
    kx = lax.div(row, gy) + gx * lax.rem(col, xl)
    kz = lax.rem(row, gy) + gy * lax.div(col, xl)
    ky = device_ref[0]

    def wave(index, length):
        folded = jnp.minimum(index, length - index)
        return folded.astype(F32) * (2.0 * math.pi / length)

    ky_all = jnp.full((8, cols), ky, jnp.int32)
    total_y = 1.0 + power(lengths_ref[2] * wave(ky_all, length_y), exponents_ref[2])
    weight = jnp.where(ky_all == 0, 1.0, 2.0)
    volume = jnp.full((8, cols), lengths_ref[0] * lengths_ref[1] * lengths_ref[2], F32)
    scale = 1.0 / (gx * xl * gy * zl * length_y)
    numerator = AMPLITUDE * jnp.sqrt(volume) * scale * weight
    total = power(lengths_ref[0] * wave(kz, gy * zl), exponents_ref[0])
    total = total + power(lengths_ref[1] * wave(kx, gx * xl), exponents_ref[1])
    gain = numerator[:1] / (total_y[:1] + total)
    data = jnp.concatenate([data_ref[pl.ds(0, rows, stride=2), :], data_ref[pl.ds(1, rows, stride=2), :]], axis=1)
    parts = split(data)
    pr, pi = left_product(outer_r, parts), left_product(outer_i, parts)
    yr, yi = pr[:, :cols] - pi[:, cols:], pr[:, cols:] + pi[:, :cols]
    data = jnp.concatenate([yr * tr - yi * ti, yr * ti + yi * tr], axis=1)
    data = right_product(split(data), (fh_ref[...], fl_ref[...]))
    data = data * jnp.concatenate([gain, gain], axis=1)
    chips = gy // 2
    count, wide = gx * chips, 2 * cols
    data = data.reshape(gx, gy, wide)
    low = data[:, :chips].reshape(count, wide)
    high = data[:, chips:].reshape(count, wide)
    data = jnp.concatenate([low[:, :cols], high[:, :cols], low[:, cols:], high[:, cols:]], axis=1)
    data = right_product(split(data), (bh_ref[...], bl_ref[...]))
    yr, yi, edge = data[:, :wide], data[:, wide : 2 * wide], data[:, 2 * wide :]
    tr, ti = br_ref[...], bi_ref[...]
    turn = edge.shape[1] // 2
    edge = edge * ea_ref[...] + pltpu.roll(edge, turn, 1) * eb_ref[...]
    parts = split(jnp.concatenate([yr * tr - yi * ti, yr * ti + yi * tr, edge], axis=1))
    pr = left_product((or_h[...], or_l[...]), parts)
    pi = left_product((oi_h[...], oi_l[...]), parts)
    lane = lax.broadcasted_iota(jnp.int32, edge.shape, 1)
    turned = pltpu.roll(pi[:, 2 * wide :], turn, 1)
    edge = pr[:, 2 * wide :] + jnp.where(lane < turn, -turned, turned)
    edge = jnp.where(lax.rem(lane, 2 * HALO) < HALO, pltpu.roll(edge, count - chips, 0), pltpu.roll(edge, chips, 0))
    out = jnp.concatenate([pr[:, :wide] - pi[:, wide : 2 * wide], pr[:, wide : 2 * wide] + pi[:, :wide], edge], axis=1)
    pieces = out.shape[1] // 128
    for piece in range(pieces):
        out_ref[pl.ds(piece, count, stride=pieces), :] = out[:, piece * 128 : (piece + 1) * 128]


def edge_rows(value, xl, low_ref, high_ref, base):
    for layer in range(value.shape[0] // xl):
        at = base + layer * HALO
        low_ref[at : at + HALO] = value[layer * xl : layer * xl + HALO]
        high_ref[at : at + HALO] = value[(layer + 1) * xl - HALO : (layer + 1) * xl]


def widen(value_ref, low_ref, high_ref, base, xl, out_ref):
    for layer in range(value_ref.shape[0] // xl):
        to, at = layer * (xl + 2 * HALO), base + layer * HALO
        out_ref[to : to + xl] = value_ref[layer * xl : (layer + 1) * xl]
        out_ref[to + xl : to + xl + HALO] = high_ref[at : at + HALO]
        out_ref[to + xl + HALO : to + xl + 2 * HALO] = low_ref[at : at + HALO]


def field_kernel(xl, device_ref, data_ref, th_ref, tl_ref, *refs):
    both_ref, own_ref, other_ref = refs[-3:]
    rows, half = th_ref.shape
    mid, count = rows // 2, half // 2
    pieces = data_ref.shape[0] // count
    data = jnp.concatenate([data_ref[pl.ds(piece, count, stride=pieces), :] for piece in range(pieces)], axis=1)
    turned = jnp.transpose(data)
    wide = (turned.shape[0] - 128) // 2
    edge = turned[2 * wide :]
    left = jnp.concatenate([turned[:wide], turned[wide : 2 * wide]], axis=1)
    edge = jnp.concatenate([edge[:64], edge[64:]], axis=1)
    core = lax.rem(device_ref[0], 2)
    at = pl.ds(pl.multiple_of(core * mid, mid), mid)
    part = right_product(split(jnp.concatenate([left, edge], axis=0)), (th_ref[at, :], tl_ref[at, :]))
    layers = wide // xl // 2
    sums = []
    for side in range(2):
        found = []
        for layer in range(side * layers, (side + 1) * layers):
            found.append(part[layer * xl : (layer + 1) * xl])
            found.append(part[wide + layer * 2 * HALO : wide + (layer + 1) * 2 * HALO])
        sums.append(jnp.concatenate(found, axis=0))
    own = jnp.where(core == 0, sums[0], sums[1])
    other = jnp.where(core == 0, sums[1], sums[0])
    size = own.shape[0]
    own_ref[...] = own
    other_ref[...] = other
    both_ref[:size] = own
    both_ref[size:] = other


def rhs_kernel(xl, gy, device_ref, recharge_ref, cells_ref, rates_ref, storage_ref, rhs_ref, low_ref, high_ref):
    rows, length = recharge_ref.shape
    wells = cells_ref.shape[1]
    at_x, at_y = lax.div(device_ref[0], gy), lax.rem(device_ref[0], gy)
    layer = cells_ref[0:1] - at_y * (rows // xl)
    line = cells_ref[1:2] - at_x * xl
    inside = (line >= 0) & (line < xl)
    at = jnp.where(inside, layer * xl + line, -1)
    rate = jnp.where(lax.broadcasted_iota(jnp.int32, (rows, wells), 0) == at, rates_ref[...], 0.0)
    column = (lax.broadcasted_iota(jnp.int32, (length, wells), 0) == cells_ref[2:3]).astype(F32).astype(BF16)
    added = None
    for _ in range(3):
        part = rate.astype(BF16)
        rate = rate - part.astype(F32)
        product = lax.dot_general(part, column, (((1,), (1,)), ((), ())), preferred_element_type=F32)
        added = product if added is None else added + product
    rhs = recharge_ref[...] + added
    rhs_ref[...] = rhs
    edge_rows(storage_ref[...], xl, low_ref, high_ref, 0)
    edge_rows(rhs, xl, low_ref, high_ref, rows // xl * HALO)


def widen_pair_kernel(xl, storage_ref, rhs_ref, low_ref, high_ref, s_ref, r_ref, first_ref, last_ref):
    layers, wide = storage_ref.shape[0] // xl, xl + 2 * HALO
    widen(storage_ref, low_ref, high_ref, 0, xl, s_ref)
    widen(rhs_ref, low_ref, high_ref, layers * HALO, xl, r_ref)
    size = (layers - 1) * wide
    first_ref[:size] = s_ref[:size]
    first_ref[size:] = r_ref[:size]
    last_ref[:size] = s_ref[wide:]
    last_ref[size:] = r_ref[wide:]


def krylov_kernel(xl, gx, gy, device_ref, both_ref, swap_ref, far_a, far_b, s_ref, r_ref, sr_low, sr_high, log_ref, u0_out, u1_out, u2_out, u3_out, diag_out, mom_out, q_all, cz, cx, cy, inv, u0, u1, u2, u3, diag):
    wide, length = xl + 2 * HALO, s_ref.shape[1]
    own = s_ref.shape[0] // wide
    total = own + 2 * HALO
    at_x, at_y = lax.div(device_ref[0], gy), lax.rem(device_ref[0], gy)
    sides = (at_y > 0, at_y < gy - 1, at_x > 0, at_x < gx - 1)
    z_lo, z_hi, x_lo, x_hi = (jnp.where(side, 1.0, 0.0) for side in sides)
    row = lax.broadcasted_iota(jnp.int32, (wide, length), 0)
    lane = lax.broadcasted_iota(jnp.int32, (wide, length), 1)
    keep_x = jnp.where(row == xl - 1, x_hi, jnp.where(row == wide - 1, x_lo, 1.0))
    keep_y = jnp.where(lane == length - 1, 0.0, 1.0)

    def at(z):
        return pl.ds(z * wide, wide)

    core = lax.rem(device_ref[0], 2)
    sign = jnp.where(core == 0, 1.0, -1.0)
    size, half = own * wide, length // 2
    first, second = slice(0, size), slice(size, 2 * size)
    full = slice(0, size)
    near = jnp.where(core == 0, 2 * size, 0)
    groups = (
        (both_ref, first, swap_ref, second, size),
        (both_ref, second, swap_ref, first, near),
        (far_a, full, far_b, full, 2 * size - near),
    )
    for group, (a_ref, a_at, b_ref, b_at, start) in enumerate(groups):
        to = pl.ds(pl.multiple_of(start, 8), size)
        a, b = a_ref[a_at], b_ref[b_at]
        lower, upper = a + b, (a - b) * sign
        q_all[to, :half] = 0.5 * jnp.exp(-lower)
        q_all[to, half:] = 0.5 * jnp.exp(-upper)
        if group == 0:
            for layer in range(own):
                log_ref[layer * xl : (layer + 1) * xl, :half] = lower[layer * wide : layer * wide + xl]
                log_ref[layer * xl : (layer + 1) * xl, half:] = upper[layer * wide : layer * wide + xl]

    def q_of(z):
        return q_all[at(z)]

    def pair_of(z):
        depth = own - 1
        if z < HALO:
            return sr_low[at(z - 1)], sr_low[at(depth + z - 1)]
        if z >= HALO + own:
            return sr_high[at(z - HALO - own)], sr_high[at(depth + z - HALO - own)]
        return s_ref[at(z - HALO)], r_ref[at(z - HALO)]

    def up_x(value):
        return pltpu.roll(value, wide - 1, 0)

    def down_x(value):
        return pltpu.roll(value, 1, 0)

    def up_y(value):
        return pltpu.roll(value, length - 1, 1)

    def down_y(value):
        return pltpu.roll(value, 1, 1)

    for z in range(total - 1):
        face = pl.reciprocal(q_of(z) + q_of(z + 1))
        if z == HALO - 1:
            face = face * z_lo
        if z == HALO + own - 1:
            face = face * z_hi
        cz[at(z)] = face
        if z == 0:
            continue
        q = q_of(z)
        storage, rhs = pair_of(z)
        face_x = pl.reciprocal(q + up_x(q)) * keep_x
        face_y = pl.reciprocal(q + up_y(q)) * keep_y
        cx[at(z)] = face_x
        cy[at(z)] = face_y
        d = storage + cz[at(z - 1)] + face + face_x + down_x(face_x) + face_y + down_y(face_y)
        inverse = pl.reciprocal(d)
        inv[at(z)] = inverse
        u0[at(z)] = rhs * inverse
        if HALO <= z < HALO + own:
            diag[pl.ds((z - HALO) * xl, xl)] = d[:xl]
    levels = (u0, u1, u2, u3)
    for level in range(3):
        old, new = levels[level], levels[level + 1]
        for z in range(2 + level, total - 2 - level):
            here, face_x, face_y = old[at(z)], cx[at(z)], cy[at(z)]
            flow = cz[at(z - 1)] * old[at(z - 1)] + cz[at(z)] * old[at(z + 1)]
            flow = flow + face_x * up_x(here) + down_x(face_x * here)
            flow = flow + face_y * up_y(here) + down_y(face_y * here)
            new[at(z)] = flow * inv[at(z)]
    sums = [None] * 6
    for z in range(HALO, HALO + own):
        to = pl.ds((z - HALO) * xl, xl)
        d = diag[to]
        values = [level[pl.ds(z * wide, xl)] for level in levels]
        for out, value in zip((u0_out, u1_out, u2_out, u3_out), values):
            out[to] = value
        diag_out[to] = d
        for i in range(6):
            if i % 2 == 0:
                weighted = d * values[i // 2]
            term = weighted * values[(i + 1) // 2]
            term = jnp.sum(term, axis=0, keepdims=True)
            sums[i] = term if sums[i] is None else sums[i] + term
    place = lax.broadcasted_iota(jnp.int32, (1, 128), 1)
    moments = jnp.zeros((1, 128), F32)
    for i in range(6):
        moments = jnp.where(place == i, jnp.sum(sums[i], axis=1, keepdims=True), moments)
    mom_out[...] = jnp.broadcast_to(moments, mom_out.shape)


def partial_kernel(in_ref, out_ref):
    out_ref[...] = jnp.broadcast_to(jnp.sum(in_ref[...], axis=0, keepdims=True), out_ref.shape)


def final_kernel(iters, mom_ref, u0, u1, u2, u3, diag_ref, pressure_ref, residual_ref):
    moments = jnp.sum(mom_ref[...], axis=0, keepdims=True)
    lane = lax.broadcasted_iota(jnp.int32, (1, 128), 1)
    nu = [jnp.sum(jnp.where(lane == i, moments, 0.0), axis=1, keepdims=True) for i in range(2 * iters)]

    def form(a, b):
        total = None
        for i, left in enumerate(a):
            for j, right in enumerate(b):
                term = left * right * nu[i + j]
                total = term if total is None else total + term
        return total

    one = jnp.ones((1, 1), F32)
    zero = jnp.zeros((1, 1), F32)
    precond, direction, pressure = [one], [one], [zero] * iters
    rz = nu[0]
    for it in range(iters):
        image = [
            (direction[i] if i < len(direction) else zero) - (direction[i - 1] if i > 0 else zero)
            for i in range(len(direction) + 1)
        ]
        alpha = rz / form(direction, image)
        pressure = [old + alpha * direction[i] if i < len(direction) else old for i, old in enumerate(pressure)]
        precond = [(precond[i] if i < len(precond) else zero) - alpha * image[i] for i in range(len(image))]
        if it + 1 < iters:
            new = form(precond, precond)
            beta = new / rz
            direction = [
                precond[i] + beta * direction[i] if i < len(direction) else precond[i] for i in range(len(precond))
            ]
            rz = new
    basis = [u0[...], u1[...], u2[...], u3[...]]
    pressure_ref[...] = pressure[0] * basis[0] + pressure[1] * basis[1] + pressure[2] * basis[2]
    total = precond[0] * basis[0] + precond[1] * basis[1] + precond[2] * basis[2] + precond[3] * basis[3]
    residual_ref[...] = diag_ref[...] * total


ITERS = 3


def exchange(low, high, axis):
    count = lax.axis_size(axis)
    up = [(i, i + 1) for i in range(count - 1)]
    down = [(i + 1, i) for i in range(count - 1)]
    from_low = lax.ppermute(high, axis, up)
    return from_low, lax.ppermute(low, axis, down)


def shards(seeds, lengths, exponents, storage, recharge, well_cells, well_rates):
    zl, xl, length_y = storage.shape
    gx, gh = lax.axis_size("gx"), lax.axis_size("gh")
    gy = 2 * gh
    assert zl == HALO and xl >= HALO
    rows, wide = zl * xl, xl + 2 * HALO
    block, middle, part = f32(rows, length_y), f32(zl * wide, length_y), f32(2 * (zl - 1) * wide, length_y)
    edge_pair = f32(2 * zl * HALO, length_y)
    at_x, at_y = lax.axis_index("gx"), lax.axis_index(("gh", "core"))
    device = (at_x * gy + at_y).reshape(1).astype(jnp.int32)
    smem = pl.BlockSpec(memory_space=pltpu.SMEM)
    vmem = pl.BlockSpec(memory_space=pltpu.VMEM)
    ty = halves(table_y(length_y))
    outer, twiddle, inner = tables_zx(gx, gy, zl, xl)
    tables = [*halves(outer.real), *halves(outer.imag), jnp.asarray(twiddle.real, F32), jnp.asarray(twiddle.imag, F32)]
    tables += [*halves(inner), *tables_back(gx, gh, zl, xl)]

    def everywhere(array, axes):
        return on_chip(lax.all_to_all(array, axes, split_axis=0, concat_axis=0, tiled=True).reshape(-1, array.shape[-1] if array.ndim == 2 else 128))

    flat_storage = storage.reshape(rows, length_y)
    rhs, low, high = call(
        lambda *refs: rhs_kernel(xl, gy, *refs),
        [block, edge_pair, edge_pair],
        device,
        recharge.reshape(rows, length_y),
        well_cells,
        well_rates.reshape(1, -1),
        flat_storage,
        specs=[smem] + [vmem] * 4,
    )
    pair_x = exchange(low, high, "gx")
    wide_storage, wide_rhs, first, last = call(
        lambda *refs: widen_pair_kernel(xl, *refs), [middle, middle, part, part], flat_storage, rhs, *pair_x
    )
    pair_low, pair_high = exchange(first, last, ("gh", "core"))

    spectrum = call(noise_kernel, f32(length_y, rows), seeds, *ty)
    spectrum = everywhere(spectrum, ("gx", "gh", "core"))
    chips, message = gx * gh, 4 * rows + 128
    spectrum = call(
        lambda *refs: spectrum_kernel((gx, gy, zl, xl, length_y), *refs),
        f32(chips * message // 128, 128),
        device,
        lengths,
        exponents,
        spectrum,
        *tables,
        specs=[smem, smem, smem] + [vmem] * (1 + len(tables)),
    )
    spectrum = everywhere(spectrum.reshape(chips, 1, message), ("gx", "gh"))
    partial = f32(zl * wide, length_y // 2)
    both, own, other = call(
        lambda *refs: field_kernel(xl, *refs),
        [f32(2 * zl * wide, length_y // 2), partial, partial],
        device,
        spectrum,
        *ty,
        first,
        specs=[smem] + [vmem] * 3 + [pl.BlockSpec(memory_space=pl.ANY)],
    )
    far = [(2 * c, 2 * c + 2) for c in range(gh - 1)] + [(2 * c + 3, 2 * c + 1) for c in range(gh - 1)]
    beside = [(2 * c + 1, 2 * c + 2) for c in range(gh - 1)] + [(2 * c + 2, 2 * c + 1) for c in range(gh - 1)]
    far_a = on_chip(lax.ppermute(other, ("gh", "core"), far))
    far_b = on_chip(lax.ppermute(own, ("gh", "core"), beside))
    swap = on_chip(lax.ppermute(both, "core", [(0, 1), (1, 0)]))

    layers = zl + 2 * HALO
    log_perm, *basis, diag, moments = call(
        lambda *refs: krylov_kernel(xl, gx, gy, *refs),
        [block] * 6 + [f32(gx, 128)],
        device,
        both,
        swap,
        far_a,
        far_b,
        wide_storage,
        wide_rhs,
        pair_low,
        pair_high,
        specs=[smem] + [vmem] * 8,
        scratch=[pltpu.VMEM((layers * wide, length_y), F32)] * 9 + [pltpu.VMEM((rows, length_y), F32)],
        limit=44,
    )
    moments = lax.all_to_all(moments, "gx", split_axis=0, concat_axis=0, tiled=True)
    moments = call(partial_kernel, f32(gy, 128), moments, limit=4)
    moments = lax.all_to_all(moments, ("gh", "core"), split_axis=0, concat_axis=0, tiled=True)
    pressure, residual = call(
        lambda *refs: final_kernel(ITERS, *refs), [block, block], moments, *map(on_chip, (*basis, diag)), limit=16
    )
    shape = storage.shape
    return (log_perm.reshape(shape), pressure.reshape(shape), residual.reshape(shape))


def solution(mesh):
    gx, gy = mesh.devices.shape
    mesh = jax.sharding.Mesh(mesh.devices.reshape(gx, gy // 2, 2), ("gx", "gh", "core"))
    z = ("gh", "core")
    block = P(z, "gx", None)
    placed = (P(z, "gx"), P(), P(), block, block, P(), P())

    return jax.shard_map(shards, mesh=mesh, in_specs=placed, out_specs=(block, block, block), check_vma=False)
```
